512 devices in a mesh: ingest: 64 (over z, y), codes: 8 (over x, core).
Axes of the slice: x: 4, y: 4, z: 16, core: 2. Of those that a mesh axis runs over, the one named last changes fastest.
Arguments:
- vectors: bfloat16 [16384, 1024], P('ingest'), may hold values from -6 to 6
- codes: int32 [8, 16384], P(None, 'ingest'), may hold values from 0 to 4095, as said below
- codebook: bfloat16 [8, 4096, 1024], P('codes', 'ingest'), may hold values from -5 to 5
- pairs: int32 [256, 64], replicated, may hold values from 0 to 255, as said below
Outputs:
- new_codebook: float32 [8, 4096, 1024], P('codes', 'ingest')
- gram: float32 [8, 4096, 8192], P('codes', 'ingest')
The draws below stay inside these ranges and needn't reach their ends.
Inputs may be any that keep to these rules, and one draw needn't show every extreme that they name: In each codebook and each aligned block of 256 vectors (the vectors of one index of ingest), at most 8 codes fall in any one range j * 64 to (j + 1) * 64 - 1; in each codebook one such range holds exactly 8 codes of every block. `pairs`: block s is codes (s % 32) * 128 to (s % 32) * 128 + 127 of codebook s // 32; every entry of row r names a block of a codebook other than that of block r; entries may repeat.
All inputs are finite; a program needn't handle non-finite values.
Results may differ from the reference program's by a relative error of at most 0.015.
Values may be sent and summed in bfloat16 or wider, within the bound.
No kernel may reach another device: no remote copies, remote signals or barrier semaphores. Data moves between devices by JAX's collectives and lax.ppermute only.
A program may use at most 64 MiB of HBM per device.

```python
import jax
import jax.numpy as jnp
from jax import lax

D = 1024
K = 4096
BLK = 128
P_SIZE = 64
VEC_DEV = 256
M = 8
VECTORS = 16384
OWN = 64
CAP = 8
KB = 32
BLOCKS = 256


def draw_codes(key, part):
    sources = VECTORS // VEC_DEV
    owners = K // OWN
    hot_key, pool_key, order_key, within_key = jax.random.split(key, 4)
    hot_range = jax.random.randint(hot_key, (M, 1, 1), 0, owners).astype(jnp.int32)
    base_pool = jnp.arange((owners - 1) * CAP, dtype=jnp.int32) // CAP

    def shuffle_pool(subkey):
        return jax.random.permutation(subkey, base_pool)

    def shuffle_order(subkey):
        return jax.random.permutation(subkey, jnp.arange(VEC_DEV, dtype=jnp.int32))
    pool_keys = jax.random.split(pool_key, M * sources)
    shuffled = jax.vmap(shuffle_pool)(pool_keys).reshape(M, sources, (owners - 1) * CAP)
    shuffled = shuffled[:, :, :VEC_DEV - CAP]
    others = (hot_range + 1 + shuffled) % owners
    labels = jnp.concatenate([jnp.broadcast_to(hot_range, (M, sources, CAP)), others], axis=2)
    order_keys = jax.random.split(order_key, M * sources)
    order = jax.vmap(shuffle_order)(order_keys).reshape(M, sources, VEC_DEV)
    labels = jnp.take_along_axis(labels, order, axis=2)
    within = jax.random.randint(within_key, (M, sources, VEC_DEV), 0, OWN).astype(jnp.int32)
    return (labels * OWN + within).reshape(M, VECTORS).astype(jnp.int32)


def draw_pairs(key, part):
    book_key, block_key = jax.random.split(key)
    row_books = (jnp.arange(BLOCKS, dtype=jnp.int32) // KB)[:, None]
    book_step = jax.random.randint(book_key, (BLOCKS, P_SIZE), 1, M).astype(jnp.int32)
    partner_book = (row_books + book_step) % M
    partner_block = jax.random.randint(block_key, (BLOCKS, P_SIZE), 0, KB).astype(jnp.int32)
    return (partner_book * KB + partner_block).astype(jnp.int32)


def block_scale(key, dims, pieces, smallest, largest):
    def one(position, blocks):
        draws = jax.random.uniform(jax.random.fold_in(jax.random.fold_in(key, 6), position), (blocks,), jnp.float32, smallest / len(pieces), largest / len(pieces))
        return jnp.repeat(jnp.exp(draws), dims[position] // blocks).reshape((-1,) + (1,) * (len(dims) - position - 1))

    gain = one(*pieces[0])
    for cut in pieces[1:]:
        gain = gain * one(*cut)
    return gain


def centred(rng, dims, deviation, limit, shards=(), held_as=jnp.bfloat16):
    values = deviation * jax.random.normal(rng, dims, jnp.float32)
    if shards:
        values = values * block_scale(rng, dims, shards, -0.22, 0.18)
    return jnp.clip(values, -limit, limit).astype(held_as)


def setup_inputs(seed: int = 0) -> dict:
    arg_keys = jax.random.split(jax.random.key(seed), 5)
    vectors = centred(arg_keys[0], (VECTORS, D), 1.0, 6.0, ((0, 64),))
    codes = draw_codes(jax.random.fold_in(arg_keys[4], 71), 0)
    codebook = centred(arg_keys[2], (M, K, D), 0.35, 5.0, ((0, 8), (1, 64)))
    pairs = draw_pairs(jax.random.fold_in(arg_keys[4], 71), 0)
    return dict(vectors=vectors, codes=codes, codebook=codebook, pairs=pairs)


def reference(vectors, codes, codebook, pairs):
    recon = jnp.zeros((VECTORS, D), jnp.float32)
    for book_index in range(M):
        recon = recon + jnp.take(codebook[book_index], codes[book_index], axis=0).astype(jnp.float32)
    residual = (vectors.astype(jnp.float32) - recon).astype(jnp.bfloat16)
    residual_wide = residual.astype(jnp.float32)
    codes_by_vector = codes.T
    slot_columns = jnp.arange(P_SIZE, dtype=jnp.int32)[None, :] * BLK

    def refit(book_global):
        own_code = lax.dynamic_index_in_dim(codes, book_global, 0, keepdims=False)
        right_side = jax.ops.segment_sum(residual_wide, own_code, num_segments=K)
        code_count = jax.ops.segment_sum(jnp.ones((VECTORS,), jnp.float32), own_code, num_segments=K)
        current = lax.dynamic_index_in_dim(codebook, book_global, 0, keepdims=False).astype(jnp.float32)
        updated = current + (right_side - 2.0 * current) / (code_count[:, None] + 2.0)
        block_id = ((book_global * K + own_code) // BLK).astype(jnp.int32)
        partner = jnp.take(pairs, block_id, axis=0)
        partner_code = jnp.take_along_axis(codes_by_vector, (partner // KB).astype(jnp.int32), axis=1)
        offset = partner_code - (partner % KB) * BLK
        valid = (offset >= 0) & (offset < BLK)
        column = (slot_columns + jnp.clip(offset, 0, BLK - 1)).astype(jnp.int32)
        weight = jnp.where(valid, 1.0, 0.0).astype(jnp.float32)
        gram_book = jnp.zeros((K, P_SIZE * BLK), jnp.float32).at[own_code[:, None], column].add(weight)
        return updated, gram_book

    new_codebook, gram = lax.map(refit, jnp.arange(M, dtype=jnp.int32))
    return new_codebook, gram
```

```python
import jax
import jax.numpy as jnp
from jax import lax
from jax.sharding import Mesh, PartitionSpec as P

K = 4096
BLK = 128
P_SIZE = 64
KB = 32
Z, Y, X, C = 16, 4, 4, 2
SIZES = {"z": Z, "y": Y, "x": X, "core": C}
CAP = 8
HALF = 32
CONTRACT_FIRST = (((0,), (0,)), ((), ()))
CONTRACT_INNER = (((1,), (0,)), ((), ()))


def pull(value, axis, step):
    size = SIZES[axis]
    return lax.ppermute(value, axis, [((i + step) % size, i) for i in range(size)])


def gather_codes(codes):
    far = jnp.stack([codes] + [pull(codes, "z", 4 * j) for j in (1, 2, 3)])
    return jnp.stack([far, pull(far, "z", 1), pull(far, "z", 2), pull(far, "z", -1)])


def gather_book(part, first, second):
    line = jnp.stack([part] + [pull(part, first, s) for s in (1, 2, 3)])
    plane = [line] + [pull(line, second, s) for s in (1, 2, 3)]
    stacked = jnp.stack(plane, axis=1 if first == "x" else 0)
    return stacked.reshape(X * Y * part.shape[0], part.shape[1])


def half_round(value):
    return value.astype(jnp.bfloat16)


def wide(value):
    return value.astype(jnp.float32)


def reconstruct(onehot, book, chain):
    partial = lax.dot_general(onehot, book, CONTRACT_FIRST, preferred_element_type=jnp.float32)
    rows = partial.shape[0] // 2
    features = partial.shape[1]
    merged = partial[:rows] + wide(pull(half_round(partial[rows:]), "core", 1))
    merged = merged.reshape(4, 4, HALF, features)
    two = half_round(merged[2])
    if chain:
        two = pull(jnp.concatenate([two[3:], two[:3]]), "z", 2)
    else:
        two = pull(two, "z", -2)
    near = merged[0] + wide(pull(half_round(merged[1]), "z", -1))
    near = near + wide(pull(half_round(merged[3]), "z", 1)) + wide(two)
    recon = near[0]
    for j in (1, 2, 3):
        recon = recon + wide(pull(half_round(near[j]), "z", -4 * j))
    return recon


def spread(residual, chain):
    far = jnp.stack([residual] + [pull(residual, "z", 4 * j) for j in (1, 2, 3)])
    if chain:
        two = pull(far, "z", -2)
        two = jnp.concatenate([two[1:], two[:1]])
    else:
        two = pull(far, "z", 2)
    own = jnp.stack([far, pull(far, "z", 1), two, pull(far, "z", -1)])
    own = own.reshape(16 * HALF, residual.shape[1])
    return jnp.concatenate([own, pull(own, "core", 1)])


def collect(onehot, residuals, first, second):
    partial = lax.dot_general(
        onehot, residuals, CONTRACT_INNER, preferred_element_type=jnp.float32
    )
    partial = partial.reshape(X, Y, -1, partial.shape[1])
    if first == "y":
        partial = jnp.swapaxes(partial, 0, 1)
    line = partial[0]
    for s in (1, 2, 3):
        line = line + wide(pull(half_round(partial[s]), first, -s))
    total = line[0]
    for s in (1, 2, 3):
        total = total + wide(pull(half_round(line[s]), second, -s))
    return total


def gram_block(all_codes, pairs, book, owner, own_rows):
    blocks, codebooks, length = all_codes.shape
    mine = lax.dynamic_index_in_dim(all_codes, book, 1, keepdims=False)
    hit = mine // own_rows == owner
    upper = (jnp.arange(length)[:, None] < jnp.arange(length)[None, :]).astype(jnp.bfloat16)
    rank = lax.dot_general(
        hit.astype(jnp.bfloat16), upper, CONTRACT_INNER, preferred_element_type=jnp.float32
    ).astype(jnp.int32)
    rank = jnp.where(hit, rank, -1)
    slots = jnp.arange(CAP, dtype=jnp.int32)
    chosen = (rank[:, None, :] == slots[None, :, None]).astype(jnp.bfloat16)
    digits = jnp.concatenate([all_codes // BLK, all_codes % BLK], axis=1).astype(jnp.bfloat16)
    packed = lax.dot_general(
        chosen, digits, (((2,), (2,)), ((0,), (0,))), preferred_element_type=jnp.float32
    ).astype(jnp.int32)
    filled = slots[None, :] < jnp.sum(hit.astype(jnp.int32), axis=1)[:, None]
    tuples = packed[:, :, :codebooks] * BLK + packed[:, :, codebooks:]
    tuples = jnp.where(filled[:, :, None], tuples, -1).reshape(blocks * CAP, codebooks)
    own_code = lax.dynamic_index_in_dim(tuples, book, 1, keepdims=False)
    local_row = own_code - owner * own_rows
    member = (local_row[:, None] == jnp.arange(own_rows, dtype=jnp.int32)).astype(jnp.bfloat16)
    code_count = jnp.sum(member, axis=0, dtype=jnp.float32)
    first_row = book * K + owner * own_rows
    partner = lax.dynamic_index_in_dim(pairs, first_row // BLK, 0, keepdims=False)
    partner_book = partner // KB
    partner_start = partner % KB * BLK
    partner_code = jnp.take(tuples, partner_book, axis=1) - partner_start[None, :]
    group = 8
    columns = []
    for g in range(P_SIZE // group):
        part = partner_code[:, g * group : (g + 1) * group]
        table = (part[:, :, None] == jnp.arange(BLK, dtype=jnp.int32)).astype(jnp.bfloat16)
        table = table.reshape(part.shape[0], group * BLK)
        columns.append(
            lax.dot_general(member, table, CONTRACT_FIRST, preferred_element_type=jnp.float32)
        )
    return jnp.concatenate(columns, axis=1), code_count


def shards(vectors, codes, codebook, pairs):
    z, y = lax.axis_index("z"), lax.axis_index("y")
    x, core = lax.axis_index("x"), lax.axis_index("core")
    codebooks, length = codes.shape
    own_rows, features = codebook.shape[1:]
    owner = z * Y + y
    book = x * C + core
    width = features // 2
    zcodes = gather_codes(codes)
    all_codes = jnp.stack([zcodes] + [pull(zcodes, "y", s) for s in (1, 2, 3)])
    portion = 2 * HALF * x
    starts = (portion + HALF * core, portion + HALF * (1 - core))
    picked = jnp.stack([lax.dynamic_slice_in_dim(zcodes, s, HALF, 3) for s in starts])
    held = [
        lax.dynamic_index_in_dim(picked, (x + s) % X * C + core, 3, keepdims=False)
        for s in range(X)
    ]
    held = jnp.stack(held).reshape(X, 2 * 16 * HALF)
    relative = jnp.where(
        held // (Y * own_rows) == z, (held - owner * own_rows) % (Y * own_rows), -1
    )
    local = jnp.arange(Y * own_rows, dtype=jnp.int32)
    onehot = (relative[:, None, :] == local[None, :, None]).astype(jnp.bfloat16)
    onehot = onehot.reshape(X * Y * own_rows, 2 * 16 * HALF)
    mine = lax.dynamic_slice_in_dim(vectors, starts[0], HALF, 0)
    orders = (("x", "y"), ("y", "x"))
    totals = []
    for chain, (first, second) in enumerate(orders):
        part = codebook[0, :, chain * width : (chain + 1) * width]
        rows = gather_book(part, first, second)
        recon = reconstruct(onehot, rows, chain)
        wanted = mine[:, chain * width : (chain + 1) * width]
        residual = half_round(wide(wanted) - recon)
        totals.append(collect(onehot, spread(residual, chain), first, second))
    right_side = jnp.concatenate(totals, axis=1)
    flat_codes = all_codes.reshape(-1, codebooks, length)
    gram, code_count = gram_block(flat_codes, pairs, book, owner, own_rows)
    current = wide(codebook[0])
    updated = current + (right_side - 2.0 * current) / (code_count[:, None] + 2.0)
    return updated[None], gram[None]


def solution(mesh):
    grid = Mesh(mesh.devices.reshape(Z, Y, X, C), ("z", "y", "x", "core"))
    rows, books = ("z", "y"), ("x", "core")
    in_specs = (P(rows, None), P(None, rows), P(books, rows, None), P())
    out_specs = (P(books, rows, None), P(books, rows, None))
    return jax.shard_map(shards, mesh=grid, in_specs=in_specs, out_specs=out_specs, check_vma=False)
```

```python
import functools

import jax
import jax.numpy as jnp
from jax import lax
from jax.experimental import pallas as pl
from jax.experimental.pallas import tpu as pltpu
from jax.sharding import Mesh, PartitionSpec as P

K = 4096
BLK = 128
P_SIZE = 64
KB = 32
Z, Y, X, C = 16, 4, 4, 2
SIZES = {"z": Z, "y": Y, "x": X, "core": C}
OWN = 64
CAP = 8
HALF = 32
PLANE = Y * OWN
CHUNK = 512
NT = (((1,), (1,)), ((), ()))
NN = (((1,), (0,)), ((), ()))


def pull(value, axis, step):
    size = SIZES[axis]
    return lax.ppermute(value, axis, [((i + step) % size, i) for i in range(size)])


def ring_pull(value):
    pairs = []
    for z in range(Z):
        pairs.append((((z + 1) % Z) * C, z * C))
        pairs.append((((z - 1) % Z) * C + 1, z * C + 1))
    return lax.ppermute(value, ("z", "core"), pairs)


def gather_codes(codes):
    held = codes[None]
    for step in (8, 4, 2, 1):
        held = jnp.concatenate([held, pull(held, "z", step)])
    by_z = held
    for step in (2, 1):
        held = jnp.concatenate([held, pull(held, "y", step)])
    return by_z, held


def gather_rows(piece):
    start = jnp.stack([piece, pull(piece, "core", 1)])
    chain = [start]
    for _ in range(7):
        chain.append(ring_pull(chain[-1]))
    last = ring_pull(chain[7][0])
    early = pull(jnp.stack(chain[1:5]), "core", 1)
    late = pull(jnp.concatenate(chain[5:8] + [last[None]]), "core", 1)
    other = [None] + [early[i] for i in range(4)] + [late[2 * i : 2 * i + 2] for i in range(3)]
    ends = (last, late[6])
    order = []
    for e in range(2):
        order += [chain[t][e] for t in range(8)] + [ends[e]]
        order += [other[16 - t][1 - e] for t in range(9, 16)]
    book = jnp.concatenate([unit[:OWN] for unit in order])
    vectors = jnp.concatenate([unit[OWN:] for unit in order])
    return book, vectors


def compact(all_codes, local):
    blocks, codebooks, length = all_codes.shape
    ranges = local // OWN
    hit = ranges[:, :, None, :] == jnp.arange(Y, dtype=jnp.int32)[None, None, :, None]
    hit = hit.reshape(blocks, X * Y, length)
    lane = jnp.arange(length)
    upper = (lane[:, None] < lane[None, :]).astype(jnp.bfloat16)
    rank = lax.dot_general(
        hit.astype(jnp.bfloat16).reshape(blocks * X * Y, length),
        upper,
        NN,
        preferred_element_type=jnp.float32,
    )
    rank = jnp.where(hit, rank.reshape(hit.shape).astype(jnp.int32), -1)
    slots = jnp.arange(CAP, dtype=jnp.int32)
    chosen = (rank[:, :, None, :] == slots[None, None, :, None]).astype(jnp.bfloat16)
    chosen = chosen.reshape(blocks, X * Y * CAP, length)
    digits = jnp.concatenate([all_codes // BLK, all_codes % BLK], axis=1).astype(jnp.bfloat16)
    packed = lax.dot_general(
        digits, chosen, (((2,), (2,)), ((0,), (0,))), preferred_element_type=jnp.float32
    ).astype(jnp.int32)
    filled = slots < jnp.sum(hit.astype(jnp.int32), axis=2)[:, :, None]
    filled = filled.reshape(blocks, 1, X * Y * CAP)
    tuples = jnp.where(filled, packed[:, :codebooks] * BLK + packed[:, codebooks:], -1)
    tuples = tuples.reshape(blocks, codebooks, X, Y * CAP)
    return tuples.transpose(2, 1, 0, 3)


def match(index_row, count):
    ids = lax.broadcasted_iota(jnp.int32, (count, index_row.shape[1]), 0)
    return jnp.where(ids == index_row, 1.0, 0.0).astype(jnp.bfloat16)


def pair_kernel(row_ref, column_ref, out_ref, total_ref):
    step = pl.program_id(1)

    @pl.when(step == 0)
    def _():
        total_ref[...] = jnp.zeros_like(total_ref)

    member = match(row_ref[0], PLANE)
    width = Z * OWN
    for e in range(C):
        table = match(column_ref[0, e : e + 1, :], width)
        span = slice(e * width, (e + 1) * width)
        total_ref[:, span] += lax.dot_general(
            member, table, NT, preferred_element_type=jnp.float32
        )

    @pl.when(step == pl.num_programs(1) - 1)
    def _():
        out_ref[0] = total_ref[...].astype(out_ref.dtype)


def pair_counts(row_index, column_index):
    books, _, slots = row_index.shape
    columns = C * Z * OWN
    return pl.pallas_call(
        pair_kernel,
        grid=(books, slots // CHUNK),
        in_specs=[
            pl.BlockSpec((1, 1, CHUNK), lambda i, s: (i, 0, s)),
            pl.BlockSpec((1, C, CHUNK), lambda i, s: (i, 0, s)),
        ],
        out_specs=pl.BlockSpec((1, PLANE, columns), lambda i, s: (i, 0, 0)),
        out_shape=jax.ShapeDtypeStruct((books, PLANE, columns), jnp.bfloat16),
        scratch_shapes=[pltpu.VMEM((PLANE, columns), jnp.float32)],
        name="pair_counts",
    )(row_index, column_index)


def gram_kernel(book_ref, start_ref, row_ref, codes_ref, out_ref):
    group = pl.program_id(0)
    member = match(row_ref[...], OWN)
    per_step = out_ref.shape[1] // BLK
    for j in range(per_step):
        p = group * per_step + j
        offset = codes_ref[pl.ds(book_ref[p], 1), :] - start_ref[p]
        out_ref[:, j * BLK : (j + 1) * BLK] = lax.dot_general(
            member, match(offset, BLK), NT, preferred_element_type=jnp.float32
        )


def gram_counts(partner_book, partner_start, row_index, tuples):
    slots = tuples.shape[1]
    width = 8 * BLK
    return pl.pallas_call(
        gram_kernel,
        grid_spec=pltpu.PrefetchScalarGridSpec(
            num_scalar_prefetch=2,
            grid=(P_SIZE * BLK // width,),
            in_specs=[
                pl.BlockSpec((1, slots), lambda g, b, s: (0, 0)),
                pl.BlockSpec(tuples.shape, lambda g, b, s: (0, 0)),
            ],
            out_specs=pl.BlockSpec((OWN, width), lambda g, b, s: (0, g)),
        ),
        out_shape=jax.ShapeDtypeStruct((OWN, P_SIZE * BLK), jnp.float32),
        name="gram_counts",
    )(partner_book, partner_start, row_index, tuples)


def by_parity(rows, core):
    shape = rows.shape
    grouped = rows.reshape(shape[:-2] + (X, C, shape[-1]))
    return lax.dynamic_index_in_dim(grouped, core, len(shape) - 1, keepdims=False)


def slot_indices(tuples, z, y, x, core):
    sign = 1 - 2 * core
    own = jnp.stack(
        [lax.dynamic_index_in_dim(tuples[i], i * C + core, 0, keepdims=True) for i in range(X)]
    )
    row_index = jnp.where(own >= 0, own - PLANE * z, -1)
    columns = []
    for e in range(C):
        book = x * C + (core + e) % C
        code = lax.dynamic_index_in_dim(tuples, book, 1, keepdims=False)
        place = ((code // PLANE - z) * sign) % Z * OWN + code % OWN
        inside = (code >= 0) & (code // OWN % Y == y)
        columns.append(jnp.where(inside, place, -1))
    return row_index, jnp.stack(columns, axis=1)


def vector_rows(by_z, z, x, core):
    codes = by_z.reshape(2, 2, 2, 2, X * C, -1).transpose(3, 2, 1, 0, 4, 5)
    codes = by_z_order(codes)
    portion = lax.dynamic_slice_in_dim(codes, 2 * HALF * x, 2 * HALF, 2)
    portion = by_parity(portion, core).reshape(Z, X, C, HALF)
    plus = portion.transpose(1, 2, 0, 3)
    minus = jnp.concatenate([portion[:1], portion[:0:-1]]).transpose(1, 2, 0, 3)[:, ::-1]
    chosen = jnp.where(core == 0, plus, minus).reshape(X, 1, C * Z * HALF)
    return chosen - PLANE * z


def by_z_order(codes):
    return codes.reshape(Z, X * C, codes.shape[-1])


def shards(vectors, codes, codebook, pairs):
    z, y = lax.axis_index("z"), lax.axis_index("y")
    x, core = lax.axis_index("x"), lax.axis_index("core")
    features = codebook.shape[2]
    owner = z * Y + y
    book = x * C + core
    mine = lax.dynamic_slice_in_dim(vectors, 2 * HALF * x + HALF * core, HALF, 0)
    by_z, all_codes = gather_codes(codes)
    rows, spread = gather_rows(jnp.concatenate([codebook[0], mine]))
    local = by_parity(all_codes, core) - PLANE * z
    tuples = compact(all_codes, local)
    tuples = tuples.reshape(X, tuples.shape[1], -1)
    row_index, column_index = slot_indices(tuples, z, y, x, core)
    counts = pair_counts(row_index, column_index).reshape(X * PLANE, -1)
    ids = jnp.arange(PLANE, dtype=jnp.int32)[None, :, None]
    assigned = (vector_rows(by_z, z, x, core) == ids).astype(jnp.bfloat16)
    assigned = assigned.reshape(X * PLANE, -1)
    partial = lax.dot_general(assigned, spread, NN, preferred_element_type=jnp.float32)
    partial -= lax.dot_general(counts, rows, NN, preferred_element_type=jnp.float32)
    sent = partial.astype(jnp.bfloat16).reshape(X * Y, OWN, features)
    received = lax.all_to_all(sent, ("x", "y"), split_axis=0, concat_axis=0, tiled=True)
    right_side = jnp.sum(received.astype(jnp.float32), axis=0)
    held = lax.dynamic_index_in_dim(tuples, x, 0, keepdims=False)
    held = held.reshape(X * C, -1, Y, CAP)
    held = lax.dynamic_index_in_dim(held, y, 2, keepdims=False).reshape(X * C, -1)
    own_row = lax.dynamic_index_in_dim(held, book, 0, keepdims=True)
    own_row = jnp.where(own_row >= 0, own_row - owner * OWN, -1)
    partner = lax.dynamic_index_in_dim(pairs, (book * K + owner * OWN) // BLK, 0, keepdims=False)
    gram = gram_counts(partner // KB, partner % KB * BLK, own_row, held)
    matched = own_row == jnp.arange(OWN, dtype=jnp.int32)[:, None]
    code_count = jnp.sum(matched.astype(jnp.float32), axis=1)
    current = codebook[0].astype(jnp.float32)
    updated = current + (right_side - 2.0 * current) / (code_count[:, None] + 2.0)
    return updated[None], gram[None]


def solution(mesh):
    grid = Mesh(mesh.devices.reshape(Z, Y, X, C), ("z", "y", "x", "core"))
    rows, books = ("z", "y"), ("x", "core")
    in_specs = (P(rows, None), P(None, rows), P(books, rows, None), P())
    out_specs = (P(books, rows, None), P(books, rows, None))
    return jax.shard_map(shards, mesh=grid, in_specs=in_specs, out_specs=out_specs, check_vma=False)
```

```python
import jax
import jax.numpy as jnp
from jax import lax
from jax.experimental import pallas as pl
from jax.experimental.pallas import tpu as pltpu
from jax.sharding import Mesh, PartitionSpec as P

K = 4096
BLK = 128
P_SIZE = 64
KB = 32
Z, Y, X, C = 16, 4, 4, 2
SIZES = {"z": Z, "y": Y, "x": X, "core": C}
OWN = 64
CAP = 8
HALF = 32
PLANE = Y * OWN
CHUNK = 512
NT = (((1,), (1,)), ((), ()))
NN = (((1,), (0,)), ((), ()))


def pull(value, axis, step):
    size = SIZES[axis]
    return lax.ppermute(value, axis, [((i + step) % size, i) for i in range(size)])


def ring_pull(value):
    pairs = []
    for z in range(Z):
        pairs.append((((z + 1) % Z) * C, z * C))
        pairs.append((((z - 1) % Z) * C + 1, z * C + 1))
    return lax.ppermute(value, ("z", "core"), pairs)


def gather_codes(codes):
    copies = jnp.broadcast_to(codes.astype(jnp.int16)[None], (Z * Y,) + codes.shape)
    return lax.all_to_all(copies, ("z", "y"), split_axis=0, concat_axis=0, tiled=True)


def gather_rows(piece):
    chain = [jnp.stack([piece, pull(piece, "core", 1)])]
    for _ in range(7):
        chain.append(ring_pull(chain[-1]))
    last = ring_pull(chain[7][0])
    early = pull(jnp.stack(chain[1:5]), "core", 1)
    late = pull(jnp.concatenate(chain[5:8] + [last[None]]), "core", 1)
    return chain, last, early, late


def unit_places():
    places = []
    for e in range(C):
        places += [(t, (e,)) for t in range(8)]
        places.append((8, ()) if e == 0 else (10, (6,)))
        for t in range(9, 16):
            back = 16 - t
            if back < 5:
                places.append((9, (back - 1, 1 - e)))
            else:
                places.append((10, (2 * (back - 5) + 1 - e,)))
    return places


def compact(all_codes, local):
    blocks, codebooks, length = all_codes.shape
    ranges = local // OWN
    hit = ranges[:, :, None, :] == jnp.arange(Y, dtype=jnp.int32)[None, None, :, None]
    hit = hit.reshape(blocks, X * Y, length)
    lane = jnp.arange(length)
    upper = (lane[:, None] < lane[None, :]).astype(jnp.bfloat16)
    rank = lax.dot_general(
        hit.astype(jnp.bfloat16).reshape(blocks * X * Y, length),
        upper,
        NN,
        preferred_element_type=jnp.float32,
    )
    rank = jnp.where(hit, rank.reshape(hit.shape).astype(jnp.int32), -1)
    slots = jnp.arange(CAP, dtype=jnp.int32)
    chosen = (rank[:, :, None, :] == slots[None, None, :, None]).astype(jnp.bfloat16)
    chosen = chosen.reshape(blocks, X * Y * CAP, length)
    ones = jnp.ones_like(all_codes[:, :1])
    digits = jnp.concatenate([all_codes // BLK, all_codes % BLK, ones], axis=1)
    digits = digits.astype(jnp.bfloat16)
    packed = lax.dot_general(
        digits, chosen, (((2,), (2,)), ((0,), (0,))), preferred_element_type=jnp.float32
    ).astype(jnp.int32)
    high, low = packed[:, :codebooks], packed[:, codebooks : 2 * codebooks]
    tuples = jnp.where(packed[:, 2 * codebooks :] > 0, high * BLK + low, -1)
    tuples = tuples.reshape(blocks, codebooks, X, Y * CAP)
    return tuples.transpose(2, 1, 0, 3)


def match(index_row, count):
    ids = lax.broadcasted_iota(jnp.int32, (count, index_row.shape[1]), 0)
    return jnp.where(ids == index_row, 1.0, 0.0).astype(jnp.bfloat16)


def pair_kernel(row_ref, column_ref, out_ref, total_ref):
    step = pl.program_id(0)

    @pl.when(step == 0)
    def _():
        total_ref[...] = jnp.zeros_like(total_ref)

    member = match(row_ref[...], PLANE)
    width = Z * OWN
    for e in range(C):
        table = match(column_ref[e : e + 1, :], width)
        span = slice(e * width, (e + 1) * width)
        total_ref[:, span] += lax.dot_general(
            member, table, NT, preferred_element_type=jnp.float32
        )

    @pl.when(step == pl.num_programs(0) - 1)
    def _():
        out_ref[...] = total_ref[...].astype(out_ref.dtype)


def pair_counts(row_index, column_index):
    slots = row_index.shape[1]
    columns = C * Z * OWN
    return pl.pallas_call(
        pair_kernel,
        grid=(slots // CHUNK,),
        in_specs=[
            pl.BlockSpec((1, CHUNK), lambda s: (0, s)),
            pl.BlockSpec((C, CHUNK), lambda s: (0, s)),
        ],
        out_specs=pl.BlockSpec((PLANE, columns), lambda s: (0, 0)),
        out_shape=jax.ShapeDtypeStruct((PLANE, columns), jnp.bfloat16),
        scratch_shapes=[pltpu.VMEM((PLANE, columns), jnp.float32)],
        cost_estimate=pl.CostEstimate(
            flops=2 * PLANE * columns * slots, transcendentals=0, bytes_accessed=1 << 20
        ),
        name="pair_counts",
    )(row_index, column_index)


def merge_kernel(*refs):
    pieces, refs = refs[:11], refs[11:]
    assigned_ref, *count_refs = refs[: 1 + X]
    out_ref, book_ref, vector_ref, sems = refs[1 + X :]
    copies = []
    for unit, (source, where) in enumerate(unit_places()):
        piece = pieces[source].at[where] if where else pieces[source]
        copies.append(
            pltpu.make_async_copy(
                piece.at[pl.ds(0, OWN)],
                book_ref.at[pl.ds(unit * OWN, OWN)],
                sems.at[2 * unit],
            )
        )
        copies.append(
            pltpu.make_async_copy(
                piece.at[pl.ds(OWN, HALF)],
                vector_ref.at[pl.ds(unit * HALF, HALF)],
                sems.at[2 * unit + 1],
            )
        )
    for copy in copies:
        copy.start()
    for copy in copies:
        copy.wait()
    for i in range(X):
        span = slice(i * PLANE, (i + 1) * PLANE)
        total = lax.dot_general(
            assigned_ref[span, :], vector_ref[...], NN, preferred_element_type=jnp.float32
        )
        total -= lax.dot_general(
            count_refs[i][...], book_ref[...], NN, preferred_element_type=jnp.float32
        )
        out_ref[span, :] = total.astype(out_ref.dtype)


def merge(chain, last, early, late, assigned, counts):
    pieces = chain + [last, early, late]
    features = last.shape[1]
    units = C * Z
    return pl.pallas_call(
        merge_kernel,
        in_specs=[pl.BlockSpec(memory_space=pl.ANY)] * len(pieces)
        + [pl.BlockSpec(memory_space=pltpu.VMEM)] * (1 + X),
        out_specs=pl.BlockSpec(memory_space=pltpu.VMEM),
        out_shape=jax.ShapeDtypeStruct((X * PLANE, features), jnp.bfloat16),
        scratch_shapes=[
            pltpu.VMEM((units * OWN, features), jnp.bfloat16),
            pltpu.VMEM((units * HALF, features), jnp.bfloat16),
            pltpu.SemaphoreType.DMA((2 * units,)),
        ],
        name="merge",
    )(*pieces, assigned, *counts)


def gram_kernel(book_ref, start_ref, row_ref, codes_ref, out_ref):
    group = pl.program_id(0)
    member = match(row_ref[...], OWN)
    per_step = out_ref.shape[1] // BLK
    for j in range(per_step):
        p = group * per_step + j
        offset = codes_ref[pl.ds(book_ref[p], 1), :] - start_ref[p]
        out_ref[:, j * BLK : (j + 1) * BLK] = lax.dot_general(
            member, match(offset, BLK), NT, preferred_element_type=jnp.float32
        )


def gram_counts(partner_book, partner_start, row_index, tuples):
    slots = tuples.shape[1]
    width = 8 * BLK
    return pl.pallas_call(
        gram_kernel,
        grid_spec=pltpu.PrefetchScalarGridSpec(
            num_scalar_prefetch=2,
            grid=(P_SIZE * BLK // width,),
            in_specs=[
                pl.BlockSpec((1, slots), lambda g, b, s: (0, 0)),
                pl.BlockSpec(tuples.shape, lambda g, b, s: (0, 0)),
            ],
            out_specs=pl.BlockSpec((OWN, width), lambda g, b, s: (0, g)),
        ),
        out_shape=jax.ShapeDtypeStruct((OWN, P_SIZE * BLK), jnp.float32),
        name="gram_counts",
    )(partner_book, partner_start, row_index, tuples)


def by_parity(rows, core):
    shape = rows.shape
    grouped = rows.reshape(shape[:-2] + (X, C, shape[-1]))
    return lax.dynamic_index_in_dim(grouped, core, len(shape) - 1, keepdims=False)


def slot_indices(tuples, z, y, x, core):
    sign = 1 - 2 * core
    own = jnp.stack(
        [lax.dynamic_index_in_dim(tuples[i], i * C + core, 0, keepdims=True) for i in range(X)]
    )
    row_index = jnp.where(own >= 0, own - PLANE * z, -1)
    columns = []
    for e in range(C):
        book = x * C + (core + e) % C
        code = lax.dynamic_index_in_dim(tuples, book, 1, keepdims=False)
        place = ((code // PLANE - z) * sign) % Z * OWN + code % OWN
        inside = (code >= 0) & (code // OWN % Y == y)
        columns.append(jnp.where(inside, place, -1))
    return row_index, jnp.stack(columns, axis=1)


def vector_rows(all_codes, z, y, x, core):
    mine = all_codes.reshape(Z, Y, X * C, -1)
    mine = lax.dynamic_index_in_dim(mine, y, 1, keepdims=False)
    portion = lax.dynamic_slice_in_dim(mine, 2 * HALF * x, 2 * HALF, 2)
    portion = by_parity(portion, core).reshape(Z, X, C, HALF)
    plus = lax.dynamic_slice_in_dim(jnp.concatenate([portion, portion]), z, Z, 0)
    back = portion[::-1]
    minus = lax.dynamic_slice_in_dim(jnp.concatenate([back, back]), Z - 1 - z, Z, 0)
    plus = plus.transpose(1, 2, 0, 3)
    minus = minus.transpose(1, 2, 0, 3)[:, ::-1]
    chosen = jnp.where(core == 0, plus, minus).reshape(X, 1, C * Z * HALF)
    return chosen - PLANE * z


def shards(vectors, codes, codebook, pairs):
    z, y = lax.axis_index("z"), lax.axis_index("y")
    x, core = lax.axis_index("x"), lax.axis_index("core")
    features = codebook.shape[2]
    owner = z * Y + y
    book = x * C + core
    mine = lax.dynamic_slice_in_dim(vectors, 2 * HALF * x + HALF * core, HALF, 0)
    pieces = gather_rows(jnp.concatenate([codebook[0], mine]))
    all_codes = gather_codes(codes).astype(jnp.int32)
    local = by_parity(all_codes, core) - PLANE * z
    tuples = compact(all_codes, local)
    tuples = tuples.reshape(X, tuples.shape[1], -1)
    row_index, column_index = slot_indices(tuples, z, y, x, core)
    counts = [pair_counts(row_index[i], column_index[i]) for i in range(X)]
    ids = jnp.arange(PLANE, dtype=jnp.int32)[None, :, None]
    assigned = (vector_rows(all_codes, z, y, x, core) == ids).astype(jnp.bfloat16)
    partial = merge(*pieces, assigned.reshape(X * PLANE, -1), counts)
    sent = partial.reshape(X * Y, OWN, features)
    received = lax.all_to_all(sent, ("x", "y"), split_axis=0, concat_axis=0, tiled=True)
    right_side = jnp.sum(received.astype(jnp.float32), axis=0)
    held = lax.dynamic_index_in_dim(tuples, x, 0, keepdims=False)
    held = held.reshape(X * C, -1, Y, CAP)
    held = lax.dynamic_index_in_dim(held, y, 2, keepdims=False).reshape(X * C, -1)
    own_row = lax.dynamic_index_in_dim(held, book, 0, keepdims=True)
    own_row = jnp.where(own_row >= 0, own_row - owner * OWN, -1)
    partner = lax.dynamic_index_in_dim(pairs, (book * K + owner * OWN) // BLK, 0, keepdims=False)
    gram = gram_counts(partner // KB, partner % KB * BLK, own_row, held)
    matched = own_row == jnp.arange(OWN, dtype=jnp.int32)[:, None]
    code_count = jnp.sum(matched.astype(jnp.float32), axis=1)
    current = codebook[0].astype(jnp.float32)
    updated = current + (right_side - 2.0 * current) / (code_count[:, None] + 2.0)
    return updated[None], gram[None]


def solution(mesh):
    grid = Mesh(mesh.devices.reshape(Z, Y, X, C), ("z", "y", "x", "core"))
    rows, books = ("z", "y"), ("x", "core")
    in_specs = (P(rows, None), P(None, rows), P(books, rows, None), P())
    out_specs = (P(books, rows, None), P(books, rows, None))
    return jax.shard_map(shards, mesh=grid, in_specs=in_specs, out_specs=out_specs, check_vma=False)
```

```python
import jax
import jax.numpy as jnp
from jax import lax
from jax.experimental import pallas as pl
from jax.experimental.pallas import tpu as pltpu
from jax.sharding import Mesh, PartitionSpec as P

K = 4096
BLK = 128
P_SIZE = 64
KB = 32
Z, Y, X, C = 16, 4, 4, 2
OWN = 64
CAP = 8
HALF = 32
PLANE = Y * OWN
CHUNK = 512
NT = (((1,), (1,)), ((), ()))
NN = (((1,), (0,)), ((), ()))


def gather_codes(codes):
    copies = jnp.broadcast_to(codes.astype(jnp.int16)[None], (Z * Y,) + codes.shape)
    return lax.all_to_all(copies, ("z", "y"), split_axis=0, concat_axis=0, tiled=True)


def compact(all_codes, local):
    blocks, codebooks, length = all_codes.shape
    ranges = local // OWN
    hit = ranges[:, :, None, :] == jnp.arange(Y, dtype=jnp.int32)[None, None, :, None]
    hit = hit.reshape(blocks, X * Y, length)
    lane = jnp.arange(length)
    upper = (lane[:, None] < lane[None, :]).astype(jnp.bfloat16)
    rank = lax.dot_general(
        hit.astype(jnp.bfloat16).reshape(blocks * X * Y, length),
        upper,
        NN,
        preferred_element_type=jnp.float32,
    )
    rank = jnp.where(hit, rank.reshape(hit.shape).astype(jnp.int32), -1)
    slots = jnp.arange(CAP, dtype=jnp.int32)
    chosen = (rank[:, :, None, :] == slots[None, None, :, None]).astype(jnp.bfloat16)
    chosen = chosen.reshape(blocks, X * Y * CAP, length)
    ones = jnp.ones_like(all_codes[:, :1])
    digits = jnp.concatenate([all_codes // BLK, all_codes % BLK, ones], axis=1)
    digits = digits.astype(jnp.bfloat16)
    packed = lax.dot_general(
        digits, chosen, (((2,), (2,)), ((0,), (0,))), preferred_element_type=jnp.float32
    ).astype(jnp.int32)
    high, low = packed[:, :codebooks], packed[:, codebooks : 2 * codebooks]
    tuples = jnp.where(packed[:, 2 * codebooks :] > 0, high * BLK + low, -1)
    tuples = tuples.reshape(blocks, codebooks, X, Y * CAP)
    return tuples.transpose(2, 1, 0, 3)


def match(index_row, count):
    ids = lax.broadcasted_iota(jnp.int32, (count, index_row.shape[1]), 0)
    return jnp.where(ids == index_row, 1.0, 0.0).astype(jnp.bfloat16)


def pair_kernel(row_ref, column_ref, out_ref, total_ref):
    step = pl.program_id(0)

    @pl.when(step == 0)
    def _():
        total_ref[...] = jnp.zeros_like(total_ref)

    member = match(row_ref[...], PLANE)
    width = Z * OWN
    for e in range(C):
        table = match(column_ref[e : e + 1, :], width)
        span = slice(e * width, (e + 1) * width)
        total_ref[:, span] += lax.dot_general(
            member, table, NT, preferred_element_type=jnp.float32
        )

    @pl.when(step == pl.num_programs(0) - 1)
    def _():
        out_ref[...] = total_ref[...].astype(out_ref.dtype)


def pair_counts(row_index, column_index):
    slots = row_index.shape[1]
    columns = C * Z * OWN
    return pl.pallas_call(
        pair_kernel,
        grid=(slots // CHUNK,),
        in_specs=[
            pl.BlockSpec((1, CHUNK), lambda s: (0, s)),
            pl.BlockSpec((C, CHUNK), lambda s: (0, s)),
        ],
        out_specs=pl.BlockSpec((PLANE, columns), lambda s: (0, 0)),
        out_shape=jax.ShapeDtypeStruct((PLANE, columns), jnp.bfloat16),
        scratch_shapes=[pltpu.VMEM((PLANE, columns), jnp.float32)],
        cost_estimate=pl.CostEstimate(
            flops=2 * PLANE * columns * slots, transcendentals=0, bytes_accessed=1 << 20
        ),
        name="pair_counts",
    )(row_index, column_index)


def merge_kernel(rows_ref, assigned_ref, *refs):
    count_refs, (out_ref, book_ref, vector_ref, total_ref, sems) = refs[:X], refs[X:]
    copies = []
    for core in range(C):
        half = rows_ref.at[:, core]
        copies.append(
            pltpu.make_async_copy(
                half.at[:, pl.ds(OWN, HALF)], vector_ref.at[core], sems.at[core]
            )
        )
    for core in range(C):
        half = rows_ref.at[:, core]
        copies.append(
            pltpu.make_async_copy(
                half.at[:, pl.ds(0, OWN)], book_ref.at[core], sems.at[C + core]
            )
        )
    for copy in copies:
        copy.start()
    features = out_ref.shape[1]
    spans = [slice(i * PLANE, (i + 1) * PLANE) for i in range(X)]
    for copy in copies[:C]:
        copy.wait()
    held = vector_ref[...].reshape(C * Z * HALF, features)
    for span in spans:
        total_ref[span, :] = lax.dot_general(
            assigned_ref[span, :], held, NN, preferred_element_type=jnp.float32
        )
    for copy in copies[C:]:
        copy.wait()
    held = book_ref[...].reshape(C * Z * OWN, features)
    for span, count_ref in zip(spans, count_refs):
        total = total_ref[span, :] - lax.dot_general(
            count_ref[...], held, NN, preferred_element_type=jnp.float32
        )
        out_ref[span, :] = total.astype(out_ref.dtype)


def merge(rows, assigned, counts):
    features = rows.shape[-1]
    whole = pl.BlockSpec(memory_space=pltpu.VMEM)
    return pl.pallas_call(
        merge_kernel,
        in_specs=[pl.BlockSpec(memory_space=pl.ANY)] + [whole] * (1 + X),
        out_specs=whole,
        out_shape=jax.ShapeDtypeStruct((X * PLANE, features), jnp.bfloat16),
        scratch_shapes=[
            pltpu.VMEM((C, Z, OWN, features), jnp.bfloat16),
            pltpu.VMEM((C, Z, HALF, features), jnp.bfloat16),
            pltpu.VMEM((X * PLANE, features), jnp.float32),
            pltpu.SemaphoreType.DMA((2 * C,)),
        ],
        name="merge",
    )(rows, assigned, *counts)


def gram_kernel(book_ref, start_ref, row_ref, codes_ref, out_ref):
    group = pl.program_id(0)
    member = match(row_ref[...], OWN)
    per_step = out_ref.shape[1] // BLK
    for j in range(per_step):
        p = group * per_step + j
        offset = codes_ref[pl.ds(book_ref[p], 1), :] - start_ref[p]
        out_ref[:, j * BLK : (j + 1) * BLK] = lax.dot_general(
            member, match(offset, BLK), NT, preferred_element_type=jnp.float32
        )


def gram_counts(partner_book, partner_start, row_index, tuples):
    slots = tuples.shape[1]
    width = 8 * BLK
    return pl.pallas_call(
        gram_kernel,
        grid_spec=pltpu.PrefetchScalarGridSpec(
            num_scalar_prefetch=2,
            grid=(P_SIZE * BLK // width,),
            in_specs=[
                pl.BlockSpec((1, slots), lambda g, b, s: (0, 0)),
                pl.BlockSpec(tuples.shape, lambda g, b, s: (0, 0)),
            ],
            out_specs=pl.BlockSpec((OWN, width), lambda g, b, s: (0, g)),
        ),
        out_shape=jax.ShapeDtypeStruct((OWN, P_SIZE * BLK), jnp.float32),
        name="gram_counts",
    )(partner_book, partner_start, row_index, tuples)


def by_parity(rows, core):
    shape = rows.shape
    grouped = rows.reshape(shape[:-2] + (X, C, shape[-1]))
    return lax.dynamic_index_in_dim(grouped, core, len(shape) - 1, keepdims=False)


def slot_indices(tuples, z, y, x, core):
    own = jnp.stack(
        [lax.dynamic_index_in_dim(tuples[i], i * C + core, 0, keepdims=True) for i in range(X)]
    )
    row_index = jnp.where(own >= 0, own - PLANE * z, -1)
    code = lax.dynamic_slice_in_dim(tuples, x * C, C, 1)
    place = code // PLANE * OWN + code % OWN
    inside = (code >= 0) & (code // OWN % Y == y)
    return row_index, jnp.where(inside, place, -1)


def vector_rows(all_codes, z, y, x, core):
    mine = all_codes.reshape(Z, Y, X * C, -1)
    mine = lax.dynamic_index_in_dim(mine, y, 1, keepdims=False)
    portion = lax.dynamic_slice_in_dim(mine, C * HALF * x, C * HALF, 2)
    portion = by_parity(portion, core).reshape(Z, X, C, HALF)
    return portion.transpose(1, 2, 0, 3).reshape(X, 1, C * Z * HALF) - PLANE * z


def shards(vectors, codes, codebook, pairs):
    z, y = lax.axis_index("z"), lax.axis_index("y")
    x, core = lax.axis_index("x"), lax.axis_index("core")
    features = codebook.shape[2]
    owner = z * Y + y
    book = x * C + core
    mine = lax.dynamic_slice_in_dim(vectors, 2 * HALF * x + HALF * core, HALF, 0)
    piece = jnp.concatenate([codebook[0], mine])
    rows = lax.all_gather(piece, ("z", "core")).reshape(Z, C, OWN + HALF, features)
    all_codes = gather_codes(codes).astype(jnp.int32)
    local = by_parity(all_codes, core) - PLANE * z
    tuples = compact(all_codes, local)
    tuples = tuples.reshape(X, tuples.shape[1], -1)
    row_index, column_index = slot_indices(tuples, z, y, x, core)
    ids = jnp.arange(PLANE, dtype=jnp.int32)[None, :, None]
    assigned = (vector_rows(all_codes, z, y, x, core) == ids).astype(jnp.bfloat16)
    assigned = assigned.reshape(X * PLANE, -1)
    counts = [pair_counts(row_index[i], column_index[i]) for i in range(X)]
    held = lax.dynamic_index_in_dim(tuples, x, 0, keepdims=False)
    held = held.reshape(X * C, -1, Y, CAP)
    held = lax.dynamic_index_in_dim(held, y, 2, keepdims=False).reshape(X * C, -1)
    own_row = lax.dynamic_index_in_dim(held, book, 0, keepdims=True)
    own_row = jnp.where(own_row >= 0, own_row - owner * OWN, -1)
    partner = lax.dynamic_index_in_dim(pairs, (book * K + owner * OWN) // BLK, 0, keepdims=False)
    gram = gram_counts(partner // KB, partner % KB * BLK, own_row, held)
    matched = own_row == jnp.arange(OWN, dtype=jnp.int32)[:, None]
    code_count = jnp.sum(matched.astype(jnp.float32), axis=1)
    assigned, gram, code_count = lax.optimization_barrier((assigned, gram, code_count))
    partial = merge(rows, assigned, counts).reshape(X * Y, OWN, features)
    received = lax.all_to_all(partial, ("x", "y"), split_axis=0, concat_axis=0, tiled=True)
    right_side = jnp.sum(received.astype(jnp.float32), axis=0)
    current = codebook[0].astype(jnp.float32)
    updated = current + (right_side - 2.0 * current) / (code_count[:, None] + 2.0)
    return updated[None], gram[None]


def solution(mesh):
    grid = Mesh(mesh.devices.reshape(Z, Y, X, C), ("z", "y", "x", "core"))
    rows, books = ("z", "y"), ("x", "core")
    in_specs = (P(rows, None), P(None, rows), P(books, rows, None), P())
    out_specs = (P(books, rows, None), P(books, rows, None))
    return jax.shard_map(shards, mesh=grid, in_specs=in_specs, out_specs=out_specs, check_vma=False)
```

```python
import jax
import jax.numpy as jnp
from jax import lax
from jax.experimental import pallas as pl
from jax.experimental.pallas import tpu as pltpu
from jax.sharding import Mesh, PartitionSpec as P

K = 4096
BLK = 128
P_SIZE = 64
KB = 32
Z, Y, X, C = 16, 4, 4, 2
OWN = 64
CAP = 8
HALF = 32
PLANE = Y * OWN
CHUNK = 512
PARTS = 4
NT = (((1,), (1,)), ((), ()))
NN = (((1,), (0,)), ((), ()))


def gather_codes(codes, book):
    mine = lax.dynamic_slice_in_dim(codes.astype(jnp.int16), book, 1, 0)
    copies = jnp.broadcast_to(mine[None], (Z * Y,) + mine.shape)
    whole = lax.all_to_all(copies, ("z", "y"), split_axis=0, concat_axis=0, tiled=True)
    whole = whole.reshape(Z * Y, codes.shape[1])
    copies = jnp.broadcast_to(whole[None], (X * C,) + whole.shape)
    books = lax.all_to_all(copies, ("x", "core"), split_axis=0, concat_axis=0, tiled=True)
    return books.astype(jnp.int32).transpose(1, 0, 2)


def compact(all_codes, local):
    blocks, codebooks, length = all_codes.shape
    ranges = local // OWN
    hit = ranges[:, :, None, :] == jnp.arange(Y, dtype=jnp.int32)[None, None, :, None]
    hit = hit.reshape(blocks, X * Y, length)
    lane = jnp.arange(length)
    upper = (lane[:, None] < lane[None, :]).astype(jnp.bfloat16)
    rank = lax.dot_general(
        hit.astype(jnp.bfloat16).reshape(blocks * X * Y, length),
        upper,
        NN,
        preferred_element_type=jnp.float32,
    )
    rank = jnp.where(hit, rank.reshape(hit.shape).astype(jnp.int32), -1)
    slots = jnp.arange(CAP, dtype=jnp.int32)
    chosen = (rank[:, :, None, :] == slots[None, None, :, None]).astype(jnp.bfloat16)
    chosen = chosen.reshape(blocks, X * Y * CAP, length)
    ones = jnp.ones_like(all_codes[:, :1])
    digits = jnp.concatenate([all_codes // BLK, all_codes % BLK, ones], axis=1)
    digits = digits.astype(jnp.bfloat16)
    packed = lax.dot_general(
        digits, chosen, (((2,), (2,)), ((0,), (0,))), preferred_element_type=jnp.float32
    ).astype(jnp.int32)
    high, low = packed[:, :codebooks], packed[:, codebooks : 2 * codebooks]
    tuples = jnp.where(packed[:, 2 * codebooks :] > 0, high * BLK + low, -1)
    tuples = tuples.reshape(blocks, codebooks, X, Y * CAP)
    return tuples.transpose(2, 1, 0, 3)


def match(index_row, count):
    ids = lax.broadcasted_iota(jnp.int32, (count, index_row.shape[1]), 0)
    return jnp.where(ids == index_row, 1.0, 0.0).astype(jnp.bfloat16)


def pair_kernel(row_ref, column_ref, out_ref, total_ref):
    step = pl.program_id(1)

    @pl.when(step == 0)
    def _():
        total_ref[...] = jnp.zeros_like(total_ref)

    member = match(row_ref[0], PLANE)
    width = Z * OWN
    for e in range(C):
        table = match(column_ref[0, e : e + 1, :], width)
        span = slice(e * width, (e + 1) * width)
        total_ref[:, span] += lax.dot_general(
            member, table, NT, preferred_element_type=jnp.float32
        )

    @pl.when(step == pl.num_programs(1) - 1)
    def _():
        out_ref[...] = total_ref[...].astype(out_ref.dtype)


def pair_counts(row_index, column_index):
    books, _, slots = row_index.shape
    columns = C * Z * OWN
    return pl.pallas_call(
        pair_kernel,
        grid=(books, slots // CHUNK),
        in_specs=[
            pl.BlockSpec((1, 1, CHUNK), lambda i, s: (i, 0, s)),
            pl.BlockSpec((1, C, CHUNK), lambda i, s: (i, 0, s)),
        ],
        out_specs=pl.BlockSpec((PLANE, columns), lambda i, s: (i, 0)),
        out_shape=jax.ShapeDtypeStruct((books * PLANE, columns), jnp.bfloat16),
        scratch_shapes=[pltpu.VMEM((PLANE, columns), jnp.float32)],
        compiler_params=pltpu.CompilerParams(vmem_limit_bytes=20 << 20),
        name="pair_counts",
    )(row_index, column_index)


def merge_kernel(
    rows_ref, counts_ref, assigned_ref, out_ref, table_ref, book_ref, vector_ref, sems
):
    features = out_ref.shape[1]
    width = features // PARTS
    tables = pltpu.make_async_copy(counts_ref, table_ref, sems.at[2 * C * PARTS])
    vectors, books = [], []
    for part in range(PARTS):
        lanes = pl.ds(part * width, width)
        for core in range(C):
            half = rows_ref.at[:, core]
            slot = (part * C + core) * 2
            vectors.append(
                pltpu.make_async_copy(
                    half.at[:, pl.ds(OWN, HALF), lanes],
                    vector_ref.at[part, core],
                    sems.at[slot],
                )
            )
            books.append(
                pltpu.make_async_copy(
                    half.at[:, pl.ds(0, OWN), lanes],
                    book_ref.at[part, core],
                    sems.at[slot + 1],
                )
            )
    for copy in vectors[:C] + [tables] + books[:C]:
        copy.start()
    for part in range(1, PARTS):
        for copy in vectors[part * C : (part + 1) * C] + books[part * C : (part + 1) * C]:
            copy.start()
    for part in range(PARTS):
        for copy in vectors[part * C : (part + 1) * C]:
            copy.wait()
        held = vector_ref[part].reshape(C * Z * HALF, width)
        total = lax.dot_general(
            assigned_ref[...], held, NN, preferred_element_type=jnp.float32
        )
        if part == 0:
            tables.wait()
        for copy in books[part * C : (part + 1) * C]:
            copy.wait()
        held = book_ref[part].reshape(C * Z * OWN, width)
        total -= lax.dot_general(
            table_ref[...], held, NN, preferred_element_type=jnp.float32
        )
        out_ref[:, part * width : (part + 1) * width] = total.astype(out_ref.dtype)


def merge(rows, assigned, counts):
    features = rows.shape[-1]
    whole = pl.BlockSpec(memory_space=pltpu.VMEM)
    placed = pl.BlockSpec(memory_space=pltpu.HBM)
    return pl.pallas_call(
        merge_kernel,
        in_specs=[placed, placed, whole],
        out_specs=whole,
        out_shape=jax.ShapeDtypeStruct((X * PLANE, features), jnp.bfloat16),
        scratch_shapes=[
            pltpu.VMEM(counts.shape, counts.dtype),
            pltpu.VMEM((PARTS, C, Z, OWN, features // PARTS), jnp.bfloat16),
            pltpu.VMEM((PARTS, C, Z, HALF, features // PARTS), jnp.bfloat16),
            pltpu.SemaphoreType.DMA((2 * C * PARTS + 1,)),
        ],
        compiler_params=pltpu.CompilerParams(vmem_limit_bytes=28 << 20),
        name="merge",
    )(*(pltpu.with_memory_space_constraint(a, pltpu.HBM) for a in (rows, counts)), assigned)


def gram_kernel(book_ref, start_ref, row_ref, codes_ref, out_ref):
    group = pl.program_id(0)
    member = match(row_ref[...], OWN)
    per_step = out_ref.shape[1] // BLK
    for j in range(per_step):
        p = group * per_step + j
        offset = codes_ref[pl.ds(book_ref[p], 1), :] - start_ref[p]
        out_ref[:, j * BLK : (j + 1) * BLK] = lax.dot_general(
            member, match(offset, BLK), NT, preferred_element_type=jnp.float32
        )


def gram_counts(partner_book, partner_start, row_index, tuples):
    slots = tuples.shape[1]
    width = 8 * BLK
    return pl.pallas_call(
        gram_kernel,
        grid_spec=pltpu.PrefetchScalarGridSpec(
            num_scalar_prefetch=2,
            grid=(P_SIZE * BLK // width,),
            in_specs=[
                pl.BlockSpec((1, slots), lambda g, b, s: (0, 0)),
                pl.BlockSpec(tuples.shape, lambda g, b, s: (0, 0)),
            ],
            out_specs=pl.BlockSpec((OWN, width), lambda g, b, s: (0, g)),
        ),
        out_shape=jax.ShapeDtypeStruct((OWN, P_SIZE * BLK), jnp.float32),
        compiler_params=pltpu.CompilerParams(vmem_limit_bytes=12 << 20),
        name="gram_counts",
    )(partner_book, partner_start, row_index, tuples)


def by_parity(rows, core):
    shape = rows.shape
    grouped = rows.reshape(shape[:-2] + (X, C, shape[-1]))
    return lax.dynamic_index_in_dim(grouped, core, len(shape) - 1, keepdims=False)


def slot_indices(tuples, z, y, x, core):
    own = jnp.stack(
        [lax.dynamic_index_in_dim(tuples[i], i * C + core, 0, keepdims=True) for i in range(X)]
    )
    row_index = jnp.where(own >= 0, own - PLANE * z, -1)
    code = lax.dynamic_slice_in_dim(tuples, x * C, C, 1)
    place = code // PLANE * OWN + code % OWN
    inside = (code >= 0) & (code // OWN % Y == y)
    return row_index, jnp.where(inside, place, -1)


def vector_rows(all_codes, z, y, x, core):
    mine = all_codes.reshape(Z, Y, X * C, -1)
    mine = lax.dynamic_index_in_dim(mine, y, 1, keepdims=False)
    portion = lax.dynamic_slice_in_dim(mine, C * HALF * x, C * HALF, 2)
    portion = by_parity(portion, core).reshape(Z, X, C, HALF)
    return portion.transpose(1, 2, 0, 3).reshape(X, 1, C * Z * HALF) - PLANE * z


def shards(vectors, codes, codebook, pairs):
    z, y = lax.axis_index("z"), lax.axis_index("y")
    x, core = lax.axis_index("x"), lax.axis_index("core")
    features = codebook.shape[2]
    owner = z * Y + y
    book = x * C + core
    mine = lax.dynamic_slice_in_dim(vectors, 2 * HALF * x + HALF * core, HALF, 0)
    piece = jnp.concatenate([codebook[0], mine])
    rows = lax.all_gather(piece, ("z", "core")).reshape(Z, C, OWN + HALF, features)
    all_codes = gather_codes(codes, book)
    local = by_parity(all_codes, core) - PLANE * z
    tuples = compact(all_codes, local)
    tuples = tuples.reshape(X, tuples.shape[1], -1)
    row_index, column_index = slot_indices(tuples, z, y, x, core)
    ids = jnp.arange(PLANE, dtype=jnp.int32)[None, :, None]
    assigned = (vector_rows(all_codes, z, y, x, core) == ids).astype(jnp.bfloat16)
    assigned = assigned.reshape(X * PLANE, -1)
    counts = pair_counts(row_index, column_index)
    held = lax.dynamic_index_in_dim(tuples, x, 0, keepdims=False)
    held = held.reshape(X * C, -1, Y, CAP)
    held = lax.dynamic_index_in_dim(held, y, 2, keepdims=False).reshape(X * C, -1)
    own_row = lax.dynamic_index_in_dim(held, book, 0, keepdims=True)
    own_row = jnp.where(own_row >= 0, own_row - owner * OWN, -1)
    partner = lax.dynamic_index_in_dim(pairs, (book * K + owner * OWN) // BLK, 0, keepdims=False)
    gram = gram_counts(partner // KB, partner % KB * BLK, own_row, held)
    matched = own_row == jnp.arange(OWN, dtype=jnp.int32)[:, None]
    code_count = jnp.sum(matched.astype(jnp.float32), axis=1)
    divisor = jnp.broadcast_to(code_count[:, None] + 2.0, (OWN, features))
    current = codebook[0].astype(jnp.float32)
    base = current - 2.0 * current / divisor
    assigned, gram, divisor, base = lax.optimization_barrier((assigned, gram, divisor, base))
    partial = merge(rows, assigned, counts).reshape(X * Y, OWN, features)
    received = lax.all_to_all(partial, ("x", "y"), split_axis=0, concat_axis=0, tiled=True)
    right_side = jnp.sum(received.astype(jnp.float32), axis=0)
    return (base + right_side / divisor)[None], gram[None]


def solution(mesh):
    grid = Mesh(mesh.devices.reshape(Z, Y, X, C), ("z", "y", "x", "core"))
    rows, books = ("z", "y"), ("x", "core")
    in_specs = (P(rows, None), P(None, rows), P(books, rows, None), P())
    out_specs = (P(books, rows, None), P(books, rows, None))
    return jax.shard_map(shards, mesh=grid, in_specs=in_specs, out_specs=out_specs, check_vma=False)
```

```python
import jax
import jax.numpy as jnp
from jax import lax
from jax.experimental import pallas as pl
from jax.experimental.pallas import tpu as pltpu
from jax.sharding import Mesh, PartitionSpec as P

K = 4096
BLK = 128
P_SIZE = 64
KB = 32
Z, Y, X, C = 16, 4, 4, 2
OWN = 64
CAP = 8
HALF = 32
PLANE = Y * OWN
NT = (((1,), (1,)), ((), ()))
NN = (((1,), (0,)), ((), ()))


def gather_codes(codes, book):
    mine = lax.dynamic_slice_in_dim(codes.astype(jnp.int16), book, 1, 0)
    copies = jnp.broadcast_to(mine[None], (Z * Y,) + mine.shape)
    whole = lax.all_to_all(copies, ("z", "y"), split_axis=0, concat_axis=0, tiled=True)
    whole = whole.reshape(Z * Y, codes.shape[1])
    copies = jnp.broadcast_to(whole[None], (X * C,) + whole.shape)
    books = lax.all_to_all(copies, ("x", "core"), split_axis=0, concat_axis=0, tiled=True)
    return books.astype(jnp.int32).transpose(1, 0, 2)


def compact(all_codes, local):
    blocks, codebooks, length = all_codes.shape
    ranges = local // OWN
    hit = ranges[:, :, None, :] == jnp.arange(Y, dtype=jnp.int32)[None, None, :, None]
    hit = hit.reshape(blocks, X * Y, length)
    lane = jnp.arange(length)
    upper = (lane[:, None] < lane[None, :]).astype(jnp.bfloat16)
    rank = lax.dot_general(
        hit.astype(jnp.bfloat16).reshape(blocks * X * Y, length),
        upper,
        NN,
        preferred_element_type=jnp.float32,
    )
    rank = jnp.where(hit, rank.reshape(hit.shape).astype(jnp.int32), -1)
    slots = jnp.arange(CAP, dtype=jnp.int32)
    chosen = (rank[:, :, None, :] == slots[None, None, :, None]).astype(jnp.bfloat16)
    chosen = chosen.reshape(blocks, X * Y * CAP, length)
    ones = jnp.ones_like(all_codes[:, :1])
    digits = jnp.concatenate([all_codes // BLK, all_codes % BLK, ones], axis=1)
    digits = digits.astype(jnp.bfloat16)
    packed = lax.dot_general(
        digits, chosen, (((2,), (2,)), ((0,), (0,))), preferred_element_type=jnp.float32
    ).astype(jnp.int32)
    high, low = packed[:, :codebooks], packed[:, codebooks : 2 * codebooks]
    tuples = jnp.where(packed[:, 2 * codebooks :] > 0, high * BLK + low, -1)
    tuples = tuples.reshape(blocks, codebooks, X, Y * CAP)
    return tuples.transpose(2, 1, 0, 3)


def match(index_row, count):
    ids = lax.broadcasted_iota(jnp.int32, (count, index_row.shape[1]), 0)
    return jnp.where(ids == index_row, 1.0, 0.0).astype(jnp.bfloat16)


def weight_kernel(row_ref, column_ref, vector_ref, out_ref):
    member = match(row_ref[0], PLANE)
    slots = member.shape[1]
    group = 4
    width = group * (OWN + HALF)
    for first in range(0, Z * C, group):
        tables = []
        for unit in range(first, first + group):
            z, core = divmod(unit, C)
            tables.append(match(column_ref[0, core : core + 1, :] - z * OWN, OWN))
            tables.append(jnp.zeros((HALF, slots), jnp.bfloat16))
        counts = lax.dot_general(
            member, jnp.concatenate(tables), NT, preferred_element_type=jnp.float32
        )
        lanes = slice(first // group * width, (first // group + 1) * width)
        assigned = match(vector_ref[0, :, lanes], PLANE).astype(jnp.float32)
        out_ref[:, lanes] = (assigned - counts).astype(out_ref.dtype)


def weights(row_index, column_index, vector_index):
    books, _, slots = row_index.shape
    columns = vector_index.shape[2]
    return pl.pallas_call(
        weight_kernel,
        grid=(books,),
        in_specs=[
            pl.BlockSpec((1, 1, slots), lambda i: (i, 0, 0)),
            pl.BlockSpec((1, C, slots), lambda i: (i, 0, 0)),
            pl.BlockSpec((1, 1, columns), lambda i: (i, 0, 0)),
        ],
        out_specs=pl.BlockSpec((PLANE, columns), lambda i: (i, 0)),
        out_shape=jax.ShapeDtypeStruct((books * PLANE, columns), jnp.bfloat16),
        compiler_params=pltpu.CompilerParams(vmem_limit_bytes=56 << 20),
        name="weights",
    )(row_index, column_index, vector_index)


def gram_kernel(book_ref, start_ref, row_ref, codes_ref, out_ref):
    group = pl.program_id(0)
    member = match(row_ref[...], OWN)
    per_step = out_ref.shape[1] // BLK
    for j in range(per_step):
        p = group * per_step + j
        offset = codes_ref[pl.ds(book_ref[p], 1), :] - start_ref[p]
        out_ref[:, j * BLK : (j + 1) * BLK] = lax.dot_general(
            member, match(offset, BLK), NT, preferred_element_type=jnp.float32
        )


def gram_counts(partner_book, partner_start, row_index, tuples):
    slots = tuples.shape[1]
    width = 8 * BLK
    return pl.pallas_call(
        gram_kernel,
        grid_spec=pltpu.PrefetchScalarGridSpec(
            num_scalar_prefetch=2,
            grid=(P_SIZE * BLK // width,),
            in_specs=[
                pl.BlockSpec((1, slots), lambda g, b, s: (0, 0)),
                pl.BlockSpec(tuples.shape, lambda g, b, s: (0, 0)),
            ],
            out_specs=pl.BlockSpec((OWN, width), lambda g, b, s: (0, g)),
        ),
        out_shape=jax.ShapeDtypeStruct((OWN, P_SIZE * BLK), jnp.float32),
        compiler_params=pltpu.CompilerParams(vmem_limit_bytes=12 << 20),
        name="gram_counts",
    )(partner_book, partner_start, row_index, tuples)


def by_parity(rows, core):
    shape = rows.shape
    grouped = rows.reshape(shape[:-2] + (X, C, shape[-1]))
    return lax.dynamic_index_in_dim(grouped, core, len(shape) - 1, keepdims=False)


def slot_indices(tuples, z, y, x, core):
    own = jnp.stack(
        [lax.dynamic_index_in_dim(tuples[i], i * C + core, 0, keepdims=True) for i in range(X)]
    )
    row_index = jnp.where(own >= 0, own - PLANE * z, -1)
    code = lax.dynamic_slice_in_dim(tuples, x * C, C, 1)
    place = code // PLANE * OWN + code % OWN
    inside = (code >= 0) & (code // OWN % Y == y)
    return row_index, jnp.where(inside, place, -1)


def vector_rows(all_codes, z, y, x, core):
    mine = all_codes.reshape(Z, Y, X * C, -1)
    mine = lax.dynamic_index_in_dim(mine, y, 1, keepdims=False)
    portion = lax.dynamic_slice_in_dim(mine, C * HALF * x, C * HALF, 2)
    portion = by_parity(portion, core).reshape(Z, X, C, HALF) - PLANE * z
    portion = jnp.pad(
        portion.transpose(1, 0, 2, 3), ((0, 0), (0, 0), (0, 0), (OWN, 0)), constant_values=-1
    )
    return portion.reshape(X, 1, Z * C * (OWN + HALF))


def shards(vectors, codes, codebook, pairs):
    z, y = lax.axis_index("z"), lax.axis_index("y")
    x, core = lax.axis_index("x"), lax.axis_index("core")
    features = codebook.shape[2]
    owner = z * Y + y
    book = x * C + core
    mine = lax.dynamic_slice_in_dim(vectors, 2 * HALF * x + HALF * core, HALF, 0)
    piece = jnp.concatenate([codebook[0], mine])
    rows = lax.all_gather(piece, ("z", "core"), tiled=True)
    all_codes = gather_codes(codes, book)
    local = by_parity(all_codes, core) - PLANE * z
    tuples = compact(all_codes, local)
    tuples = tuples.reshape(X, tuples.shape[1], -1)
    row_index, column_index = slot_indices(tuples, z, y, x, core)
    table = weights(row_index, column_index, vector_rows(all_codes, z, y, x, core))
    held = lax.dynamic_index_in_dim(tuples, x, 0, keepdims=False)
    held = held.reshape(X * C, -1, Y, CAP)
    held = lax.dynamic_index_in_dim(held, y, 2, keepdims=False).reshape(X * C, -1)
    own_row = lax.dynamic_index_in_dim(held, book, 0, keepdims=True)
    own_row = jnp.where(own_row >= 0, own_row - owner * OWN, -1)
    matched = own_row == jnp.arange(OWN, dtype=jnp.int32)[:, None]
    code_count = jnp.sum(matched.astype(jnp.float32), axis=1)
    divisor = jnp.broadcast_to(code_count[:, None] + 2.0, (OWN, features))
    current = codebook[0].astype(jnp.float32)
    base = current - 2.0 * current / divisor
    table, divisor, base = lax.optimization_barrier((table, divisor, base))
    partial = lax.dot_general(table, rows, NN, preferred_element_type=jnp.float32)
    partial = partial.astype(jnp.bfloat16)
    partial, held, own_row = lax.optimization_barrier((partial, held, own_row))
    partial = partial.reshape(X * Y, OWN, features)
    received = lax.all_to_all(partial, ("x", "y"), split_axis=0, concat_axis=0, tiled=True)
    partner = lax.dynamic_index_in_dim(pairs, (book * K + owner * OWN) // BLK, 0, keepdims=False)
    gram = gram_counts(partner // KB, partner % KB * BLK, own_row, held)
    right_side = jnp.sum(received.astype(jnp.float32), axis=0)
    return (base + right_side / divisor)[None], gram[None]


def solution(mesh):
    grid = Mesh(mesh.devices.reshape(Z, Y, X, C), ("z", "y", "x", "core"))
    rows, books = ("z", "y"), ("x", "core")
    in_specs = (P(rows, None), P(None, rows), P(books, rows, None), P())
    out_specs = (P(books, rows, None), P(books, rows, None))
    return jax.shard_map(shards, mesh=grid, in_specs=in_specs, out_specs=out_specs, check_vma=False)
```

```python
import jax
import jax.numpy as jnp
from jax import lax
from jax.experimental import pallas as pl
from jax.experimental.pallas import tpu as pltpu
from jax.sharding import Mesh, PartitionSpec as P

K = 4096
BLK = 128
P_SIZE = 64
KB = 32
Z, Y, X, C = 16, 4, 4, 2
OWN = 64
CAP = 8
PRODUCT_VMEM = 56 << 20
HALF = 32
PLANE = Y * OWN
NT = (((1,), (1,)), ((), ()))
NN = (((1,), (0,)), ((), ()))


def gather_codes(codes, book):
    mine = lax.dynamic_slice_in_dim(codes.astype(jnp.int16), book, 1, 0)
    copies = jnp.broadcast_to(mine[None], (Z * Y,) + mine.shape)
    whole = lax.all_to_all(copies, ("z", "y"), split_axis=0, concat_axis=0, tiled=True)
    whole = whole.reshape(Z * Y, codes.shape[1])
    copies = jnp.broadcast_to(whole[None], (X * C,) + whole.shape)
    books = lax.all_to_all(copies, ("x", "core"), split_axis=0, concat_axis=0, tiled=True)
    return books.astype(jnp.int32).transpose(1, 0, 2)


def compact(all_codes, local):
    blocks, codebooks, length = all_codes.shape
    ranges = local // OWN
    hit = ranges[:, :, None, :] == jnp.arange(Y, dtype=jnp.int32)[None, None, :, None]
    hit = hit.reshape(blocks, X * Y, length)
    lane = jnp.arange(length)
    upper = (lane[:, None] < lane[None, :]).astype(jnp.bfloat16)
    rank = lax.dot_general(
        hit.astype(jnp.bfloat16).reshape(blocks * X * Y, length),
        upper,
        NN,
        preferred_element_type=jnp.float32,
    )
    rank = jnp.where(hit, rank.reshape(hit.shape).astype(jnp.int32), -1)
    slots = jnp.arange(CAP, dtype=jnp.int32)
    chosen = (rank[:, :, None, :] == slots[None, None, :, None]).astype(jnp.bfloat16)
    chosen = chosen.reshape(blocks, X * Y * CAP, length)
    ones = jnp.ones_like(all_codes[:, :1])
    digits = jnp.concatenate([all_codes // BLK, all_codes % BLK, ones], axis=1)
    digits = digits.astype(jnp.bfloat16)
    packed = lax.dot_general(
        digits, chosen, (((2,), (2,)), ((0,), (0,))), preferred_element_type=jnp.float32
    ).astype(jnp.int32)
    high, low = packed[:, :codebooks], packed[:, codebooks : 2 * codebooks]
    tuples = jnp.where(packed[:, 2 * codebooks :] > 0, high * BLK + low, -1)
    tuples = tuples.reshape(blocks, codebooks, X, Y * CAP)
    return tuples.transpose(2, 1, 0, 3)


def match(index_row, count):
    ids = lax.broadcasted_iota(jnp.int32, (count, index_row.shape[1]), 0)
    return jnp.where(ids == index_row, 1.0, 0.0).astype(jnp.bfloat16)


def weight_kernel(row_ref, column_ref, vector_ref, out_ref):
    member = match(row_ref[0], PLANE)
    out_ref[...] = match(vector_ref[0], PLANE)
    for core in range(C):
        table = match(column_ref[0, core : core + 1, :], Z * OWN)
        counts = lax.dot_general(member, table, NT, preferred_element_type=jnp.float32)
        counts = (-counts).astype(out_ref.dtype)
        for z in range(Z):
            start = (z * C + core) * (OWN + HALF)
            out_ref[:, start : start + OWN] = counts[:, z * OWN : (z + 1) * OWN]


def weights(row_index, column_index, vector_index):
    books, _, slots = row_index.shape
    columns = vector_index.shape[2]
    return pl.pallas_call(
        weight_kernel,
        grid=(books,),
        in_specs=[
            pl.BlockSpec((1, 1, slots), lambda i: (i, 0, 0)),
            pl.BlockSpec((1, C, slots), lambda i: (i, 0, 0)),
            pl.BlockSpec((1, 1, columns), lambda i: (i, 0, 0)),
        ],
        out_specs=pl.BlockSpec((PLANE, columns), lambda i: (i, 0)),
        out_shape=jax.ShapeDtypeStruct((books * PLANE, columns), jnp.bfloat16),
        compiler_params=pltpu.CompilerParams(vmem_limit_bytes=56 << 20),
        name="weights",
    )(row_index, column_index, vector_index)


def product_kernel(left_ref, right_ref, out_ref):
    total = lax.dot_general(
        left_ref[...], right_ref[...], NN, preferred_element_type=jnp.float32
    )
    out_ref[...] = total.astype(out_ref.dtype)


def product(left, right):
    rows, depth = left.shape
    features = right.shape[1]
    width = features // 4
    return pl.pallas_call(
        product_kernel,
        grid=(features // width,),
        in_specs=[
            pl.BlockSpec((rows, depth), lambda n: (0, 0)),
            pl.BlockSpec((depth, width), lambda n: (0, n)),
        ],
        out_specs=pl.BlockSpec((rows, width), lambda n: (0, n)),
        out_shape=jax.ShapeDtypeStruct((rows, features), jnp.bfloat16),
        compiler_params=pltpu.CompilerParams(vmem_limit_bytes=PRODUCT_VMEM),
        name="product",
    )(left, right)


def piece_kernel(index_ref, book_ref, vector_ref, out_ref):
    out_ref[:OWN, :] = book_ref[...]
    out_ref[OWN:, :] = vector_ref[...]


def make_piece(book_rows, vectors, index):
    features = vectors.shape[1]
    return pl.pallas_call(
        piece_kernel,
        grid_spec=pltpu.PrefetchScalarGridSpec(
            num_scalar_prefetch=1,
            grid=(1,),
            in_specs=[
                pl.BlockSpec((OWN, features), lambda i, n: (0, 0)),
                pl.BlockSpec((HALF, features), lambda i, n: (n[0], 0)),
            ],
            out_specs=pl.BlockSpec((OWN + HALF, features), lambda i, n: (0, 0)),
        ),
        out_shape=jax.ShapeDtypeStruct((OWN + HALF, features), jnp.bfloat16),
        compiler_params=pltpu.CompilerParams(vmem_limit_bytes=4 << 20),
        name="make_piece",
    )(index, book_rows, vectors)


def gram_kernel(book_ref, start_ref, row_ref, codes_ref, out_ref):
    group = pl.program_id(0)
    member = match(row_ref[...], OWN)
    per_step = out_ref.shape[1] // BLK
    for j in range(per_step):
        p = group * per_step + j
        offset = codes_ref[pl.ds(book_ref[p], 1), :] - start_ref[p]
        out_ref[:, j * BLK : (j + 1) * BLK] = lax.dot_general(
            member, match(offset, BLK), NT, preferred_element_type=jnp.float32
        )


def gram_counts(partner_book, partner_start, row_index, tuples):
    slots = tuples.shape[1]
    width = 8 * BLK
    return pl.pallas_call(
        gram_kernel,
        grid_spec=pltpu.PrefetchScalarGridSpec(
            num_scalar_prefetch=2,
            grid=(P_SIZE * BLK // width,),
            in_specs=[
                pl.BlockSpec((1, slots), lambda g, b, s: (0, 0)),
                pl.BlockSpec(tuples.shape, lambda g, b, s: (0, 0)),
            ],
            out_specs=pl.BlockSpec((OWN, width), lambda g, b, s: (0, g)),
        ),
        out_shape=jax.ShapeDtypeStruct((OWN, P_SIZE * BLK), jnp.float32),
        compiler_params=pltpu.CompilerParams(vmem_limit_bytes=12 << 20),
        name="gram_counts",
    )(partner_book, partner_start, row_index, tuples)


def by_parity(rows, core):
    shape = rows.shape
    grouped = rows.reshape(shape[:-2] + (X, C, shape[-1]))
    return lax.dynamic_index_in_dim(grouped, core, len(shape) - 1, keepdims=False)


def slot_indices(tuples, z, y, x, core):
    own = jnp.stack(
        [lax.dynamic_index_in_dim(tuples[i], i * C + core, 0, keepdims=True) for i in range(X)]
    )
    row_index = jnp.where(own >= 0, own - PLANE * z, -1)
    code = lax.dynamic_slice_in_dim(tuples, x * C, C, 1)
    place = code // PLANE * OWN + code % OWN
    inside = (code >= 0) & (code // OWN % Y == y)
    return row_index, jnp.where(inside, place, -1)


def vector_rows(all_codes, z, y, x, core):
    mine = all_codes.reshape(Z, Y, X * C, -1)
    mine = lax.dynamic_index_in_dim(mine, y, 1, keepdims=False)
    portion = lax.dynamic_slice_in_dim(mine, C * HALF * x, C * HALF, 2)
    portion = by_parity(portion, core).reshape(Z, X, C, HALF) - PLANE * z
    portion = jnp.pad(
        portion.transpose(1, 0, 2, 3), ((0, 0), (0, 0), (0, 0), (OWN, 0)), constant_values=-1
    )
    return portion.reshape(X, 1, Z * C * (OWN + HALF))


def shards(vectors, codes, codebook, pairs):
    z, y = lax.axis_index("z"), lax.axis_index("y")
    x, core = lax.axis_index("x"), lax.axis_index("core")
    features = codebook.shape[2]
    owner = z * Y + y
    book = x * C + core
    stored = (pltpu.with_memory_space_constraint(a, pltpu.HBM) for a in (codebook[0], vectors))
    piece = make_piece(*stored, book.astype(jnp.int32)[None])
    rows = lax.all_gather(piece, ("z", "core"), tiled=True)
    all_codes = gather_codes(codes, book)
    local = by_parity(all_codes, core) - PLANE * z
    tuples = compact(all_codes, local)
    tuples = tuples.reshape(X, tuples.shape[1], -1)
    row_index, column_index = slot_indices(tuples, z, y, x, core)
    table = weights(row_index, column_index, vector_rows(all_codes, z, y, x, core))
    held = lax.dynamic_index_in_dim(tuples, x, 0, keepdims=False)
    held = held.reshape(X * C, -1, Y, CAP)
    held = lax.dynamic_index_in_dim(held, y, 2, keepdims=False).reshape(X * C, -1)
    own_row = lax.dynamic_index_in_dim(held, book, 0, keepdims=True)
    own_row = jnp.where(own_row >= 0, own_row - owner * OWN, -1)
    matched = own_row == jnp.arange(OWN, dtype=jnp.int32)[:, None]
    code_count = jnp.sum(matched.astype(jnp.float32), axis=1)
    divisor = jnp.broadcast_to(code_count[:, None] + 2.0, (OWN, features))
    current = codebook[0].astype(jnp.float32)
    base = current - 2.0 * current / divisor
    table, divisor, base = lax.optimization_barrier((table, divisor, base))
    partial = product(table, rows)
    partial, held, own_row = lax.optimization_barrier((partial, held, own_row))
    partial = partial.reshape(X * Y, OWN, features)
    received = lax.all_to_all(partial, ("x", "y"), split_axis=0, concat_axis=0, tiled=True)
    partner = lax.dynamic_index_in_dim(pairs, (book * K + owner * OWN) // BLK, 0, keepdims=False)
    gram = gram_counts(partner // KB, partner % KB * BLK, own_row, held)
    right_side = jnp.sum(received.astype(jnp.float32), axis=0)
    return (base + right_side / divisor)[None], gram[None]


def solution(mesh):
    grid = Mesh(mesh.devices.reshape(Z, Y, X, C), ("z", "y", "x", "core"))
    rows, books = ("z", "y"), ("x", "core")
    in_specs = (P(rows, None), P(None, rows), P(books, rows, None), P())
    out_specs = (P(books, rows, None), P(books, rows, None))
    return jax.shard_map(shards, mesh=grid, in_specs=in_specs, out_specs=out_specs, check_vma=False)
```

```python
import jax
import jax.numpy as jnp
from jax import lax
from jax.experimental import pallas as pl
from jax.experimental.pallas import tpu as pltpu
from jax.sharding import Mesh, PartitionSpec as P

K = 4096
BLK = 128
P_SIZE = 64
KB = 32
Z, Y, X, C = 16, 4, 4, 2
OWN = 64
CAP = 8
BANDS = 4
HALF = 32
PLANE = Y * OWN
NT = (((1,), (1,)), ((), ()))
NN = (((1,), (0,)), ((), ()))


def gather_codes(codes, book):
    mine = lax.dynamic_slice_in_dim(codes.astype(jnp.int16), book, 1, 0)
    copies = jnp.broadcast_to(mine[None], (Z * Y,) + mine.shape)
    whole = lax.all_to_all(copies, ("z", "y"), split_axis=0, concat_axis=0, tiled=True)
    whole = whole.reshape(Z * Y, codes.shape[1])
    copies = jnp.broadcast_to(whole[None], (X * C,) + whole.shape)
    books = lax.all_to_all(copies, ("x", "core"), split_axis=0, concat_axis=0, tiled=True)
    return books.astype(jnp.int32).transpose(1, 0, 2)


def compact(all_codes, local):
    blocks, codebooks, length = all_codes.shape
    ranges = local // OWN
    hit = ranges[:, :, None, :] == jnp.arange(Y, dtype=jnp.int32)[None, None, :, None]
    hit = hit.reshape(blocks, X * Y, length)
    lane = jnp.arange(length)
    upper = (lane[:, None] < lane[None, :]).astype(jnp.bfloat16)
    rank = lax.dot_general(
        hit.astype(jnp.bfloat16).reshape(blocks * X * Y, length),
        upper,
        NN,
        preferred_element_type=jnp.float32,
    )
    rank = jnp.where(hit, rank.reshape(hit.shape).astype(jnp.int32), -1)
    slots = jnp.arange(CAP, dtype=jnp.int32)
    chosen = (rank[:, :, None, :] == slots[None, None, :, None]).astype(jnp.bfloat16)
    chosen = chosen.reshape(blocks, X * Y * CAP, length)
    ones = jnp.ones_like(all_codes[:, :1])
    digits = jnp.concatenate([all_codes // BLK, all_codes % BLK, ones], axis=1)
    digits = digits.astype(jnp.bfloat16)
    packed = lax.dot_general(
        digits, chosen, (((2,), (2,)), ((0,), (0,))), preferred_element_type=jnp.float32
    ).astype(jnp.int32)
    high, low = packed[:, :codebooks], packed[:, codebooks : 2 * codebooks]
    tuples = jnp.where(packed[:, 2 * codebooks :] > 0, high * BLK + low, -1)
    tuples = tuples.reshape(blocks, codebooks, X, Y * CAP)
    return tuples.transpose(2, 1, 0, 3)


def match(index_row, count):
    ids = lax.broadcasted_iota(jnp.int32, (count, index_row.shape[1]), 0)
    return jnp.where(ids == index_row, 1.0, 0.0).astype(jnp.bfloat16)


def weight_kernel(row_ref, column_ref, vector_ref, out_ref):
    member = match(row_ref[0], PLANE)
    out_ref[...] = match(vector_ref[0], PLANE)
    for core in range(C):
        table = match(column_ref[0, core : core + 1, :], Z * OWN)
        counts = lax.dot_general(member, table, NT, preferred_element_type=jnp.float32)
        counts = (-counts).astype(out_ref.dtype)
        for z in range(Z):
            start = (z * C + core) * (OWN + HALF)
            out_ref[:, start : start + OWN] = counts[:, z * OWN : (z + 1) * OWN]


def weights(row_index, column_index, vector_index):
    books, _, slots = row_index.shape
    columns = vector_index.shape[2]
    return pl.pallas_call(
        weight_kernel,
        grid=(books,),
        in_specs=[
            pl.BlockSpec((1, 1, slots), lambda i: (i, 0, 0)),
            pl.BlockSpec((1, C, slots), lambda i: (i, 0, 0)),
            pl.BlockSpec((1, 1, columns), lambda i: (i, 0, 0)),
        ],
        out_specs=pl.BlockSpec((PLANE, columns), lambda i: (i, 0)),
        out_shape=jax.ShapeDtypeStruct((books * PLANE, columns), jnp.bfloat16),
        compiler_params=pltpu.CompilerParams(vmem_limit_bytes=56 << 20),
        name="weights",
    )(row_index, column_index, vector_index)


def product_kernel(left_ref, right_ref, out_ref, table_ref, rows_ref, sems):
    parts, _, width = rows_ref.shape
    height = table_ref.shape[0] // BANDS
    bands = [slice(m * height, (m + 1) * height) for m in range(BANDS)]
    tables = [
        pltpu.make_async_copy(
            left_ref.at[pl.ds(m * height, height)],
            table_ref.at[pl.ds(m * height, height)],
            sems.at[m],
        )
        for m in range(BANDS)
    ]
    rows = [
        pltpu.make_async_copy(
            right_ref.at[:, pl.ds(n * width, width)], rows_ref.at[n], sems.at[BANDS + n]
        )
        for n in range(parts)
    ]
    for copy in rows[:1] + tables + rows[1:]:
        copy.start()
    for n in range(parts):
        rows[n].wait()
        for m, band in enumerate(bands):
            if n == 0:
                tables[m].wait()
            total = lax.dot_general(
                table_ref[band, :], rows_ref[n], NN, preferred_element_type=jnp.float32
            )
            out_ref[band, n * width : (n + 1) * width] = total.astype(out_ref.dtype)


def product(left, right):
    features = right.shape[1]
    parts = 2
    left, right = (pltpu.with_memory_space_constraint(a, pltpu.HBM) for a in (left, right))
    return pl.pallas_call(
        product_kernel,
        in_specs=[pl.BlockSpec(memory_space=pltpu.HBM)] * 2,
        out_specs=pl.BlockSpec(memory_space=pltpu.VMEM),
        out_shape=jax.ShapeDtypeStruct((left.shape[0], features), jnp.bfloat16),
        scratch_shapes=[
            pltpu.VMEM(left.shape, left.dtype),
            pltpu.VMEM((parts, right.shape[0], features // parts), right.dtype),
            pltpu.SemaphoreType.DMA((BANDS + parts,)),
        ],
        compiler_params=pltpu.CompilerParams(vmem_limit_bytes=32 << 20),
        name="product",
    )(left, right)


def piece_kernel(index_ref, book_ref, vector_ref, out_ref):
    out_ref[:OWN, :] = book_ref[...]
    out_ref[OWN:, :] = vector_ref[...]


def make_piece(book_rows, vectors, index):
    features = vectors.shape[1]
    return pl.pallas_call(
        piece_kernel,
        grid_spec=pltpu.PrefetchScalarGridSpec(
            num_scalar_prefetch=1,
            grid=(1,),
            in_specs=[
                pl.BlockSpec((OWN, features), lambda i, n: (0, 0)),
                pl.BlockSpec((HALF, features), lambda i, n: (n[0], 0)),
            ],
            out_specs=pl.BlockSpec((OWN + HALF, features), lambda i, n: (0, 0)),
        ),
        out_shape=jax.ShapeDtypeStruct((OWN + HALF, features), jnp.bfloat16),
        compiler_params=pltpu.CompilerParams(vmem_limit_bytes=4 << 20),
        name="make_piece",
    )(index, book_rows, vectors)


def gram_kernel(book_ref, start_ref, row_ref, codes_ref, out_ref):
    group = pl.program_id(0)
    member = match(row_ref[...], OWN)
    per_step = out_ref.shape[1] // BLK
    for j in range(per_step):
        p = group * per_step + j
        offset = codes_ref[pl.ds(book_ref[p], 1), :] - start_ref[p]
        out_ref[:, j * BLK : (j + 1) * BLK] = lax.dot_general(
            member, match(offset, BLK), NT, preferred_element_type=jnp.float32
        )


def gram_counts(partner_book, partner_start, row_index, tuples):
    slots = tuples.shape[1]
    width = 8 * BLK
    return pl.pallas_call(
        gram_kernel,
        grid_spec=pltpu.PrefetchScalarGridSpec(
            num_scalar_prefetch=2,
            grid=(P_SIZE * BLK // width,),
            in_specs=[
                pl.BlockSpec((1, slots), lambda g, b, s: (0, 0)),
                pl.BlockSpec(tuples.shape, lambda g, b, s: (0, 0)),
            ],
            out_specs=pl.BlockSpec((OWN, width), lambda g, b, s: (0, g)),
        ),
        out_shape=jax.ShapeDtypeStruct((OWN, P_SIZE * BLK), jnp.float32),
        compiler_params=pltpu.CompilerParams(vmem_limit_bytes=12 << 20),
        name="gram_counts",
    )(partner_book, partner_start, row_index, tuples)


def by_parity(rows, core):
    shape = rows.shape
    grouped = rows.reshape(shape[:-2] + (X, C, shape[-1]))
    return lax.dynamic_index_in_dim(grouped, core, len(shape) - 1, keepdims=False)


def slot_indices(tuples, z, y, x, core):
    own = jnp.stack(
        [lax.dynamic_index_in_dim(tuples[i], i * C + core, 0, keepdims=True) for i in range(X)]
    )
    row_index = jnp.where(own >= 0, own - PLANE * z, -1)
    code = lax.dynamic_slice_in_dim(tuples, x * C, C, 1)
    place = code // PLANE * OWN + code % OWN
    inside = (code >= 0) & (code // OWN % Y == y)
    return row_index, jnp.where(inside, place, -1)


def vector_rows(all_codes, z, y, x, core):
    mine = all_codes.reshape(Z, Y, X * C, -1)
    mine = lax.dynamic_index_in_dim(mine, y, 1, keepdims=False)
    portion = lax.dynamic_slice_in_dim(mine, C * HALF * x, C * HALF, 2)
    portion = by_parity(portion, core).reshape(Z, X, C, HALF) - PLANE * z
    portion = jnp.pad(
        portion.transpose(1, 0, 2, 3), ((0, 0), (0, 0), (0, 0), (OWN, 0)), constant_values=-1
    )
    return portion.reshape(X, 1, Z * C * (OWN + HALF))


def shards(vectors, codes, codebook, pairs):
    z, y = lax.axis_index("z"), lax.axis_index("y")
    x, core = lax.axis_index("x"), lax.axis_index("core")
    features = codebook.shape[2]
    owner = z * Y + y
    book = x * C + core
    stored = (pltpu.with_memory_space_constraint(a, pltpu.HBM) for a in (codebook[0], vectors))
    piece = make_piece(*stored, book.astype(jnp.int32)[None])
    rows = lax.all_gather(piece, ("z", "core"), tiled=True)
    all_codes = gather_codes(codes, book)
    local = by_parity(all_codes, core) - PLANE * z
    tuples = compact(all_codes, local)
    tuples = tuples.reshape(X, tuples.shape[1], -1)
    row_index, column_index = slot_indices(tuples, z, y, x, core)
    table = weights(row_index, column_index, vector_rows(all_codes, z, y, x, core))
    held = lax.dynamic_index_in_dim(tuples, x, 0, keepdims=False)
    held = held.reshape(X * C, -1, Y, CAP)
    held = lax.dynamic_index_in_dim(held, y, 2, keepdims=False).reshape(X * C, -1)
    own_row = lax.dynamic_index_in_dim(held, book, 0, keepdims=True)
    own_row = jnp.where(own_row >= 0, own_row - owner * OWN, -1)
    matched = own_row == jnp.arange(OWN, dtype=jnp.int32)[:, None]
    code_count = jnp.sum(matched.astype(jnp.float32), axis=1)
    divisor = jnp.broadcast_to(code_count[:, None] + 2.0, (OWN, features))
    current = codebook[0].astype(jnp.float32)
    base = current - 2.0 * current / divisor
    partner = lax.dynamic_index_in_dim(pairs, (book * K + owner * OWN) // BLK, 0, keepdims=False)
    gram = gram_counts(partner // KB, partner % KB * BLK, own_row, held)
    table, gram, divisor, base = lax.optimization_barrier((table, gram, divisor, base))
    partial = product(table, rows)
    partial = partial.reshape(X * Y, OWN, features)
    received = lax.all_to_all(partial, ("x", "y"), split_axis=0, concat_axis=0, tiled=True)
    right_side = jnp.sum(received.astype(jnp.float32), axis=0)
    return (base + right_side / divisor)[None], gram[None]


def solution(mesh):
    grid = Mesh(mesh.devices.reshape(Z, Y, X, C), ("z", "y", "x", "core"))
    rows, books = ("z", "y"), ("x", "core")
    in_specs = (P(rows, None), P(None, rows), P(books, rows, None), P())
    out_specs = (P(books, rows, None), P(books, rows, None))
    return jax.shard_map(shards, mesh=grid, in_specs=in_specs, out_specs=out_specs, check_vma=False)
```

```python
import jax
import jax.numpy as jnp
from jax import lax
from jax.experimental import pallas as pl
from jax.experimental.pallas import tpu as pltpu
from jax.sharding import Mesh, PartitionSpec as P

K = 4096
BLK = 128
P_SIZE = 64
KB = 32
Z, Y, X, C = 16, 4, 4, 2
OWN = 64
CAP = 8
BANDS = 4
HALF = 32
PLANE = Y * OWN
NT = (((1,), (1,)), ((), ()))
NN = (((1,), (0,)), ((), ()))


def gather_codes(codes, book):
    mine = lax.dynamic_slice_in_dim(codes.astype(jnp.int16), book, 1, 0)
    copies = jnp.broadcast_to(mine[None], (Z * Y,) + mine.shape)
    whole = lax.all_to_all(copies, ("z", "y"), split_axis=0, concat_axis=0, tiled=True)
    whole = whole.reshape(Z * Y, codes.shape[1])
    copies = jnp.broadcast_to(whole[None], (X * C,) + whole.shape)
    books = lax.all_to_all(copies, ("x", "core"), split_axis=0, concat_axis=0, tiled=True)
    return books.astype(jnp.int32).transpose(1, 0, 2)


def compact(all_codes, local):
    blocks, codebooks, length = all_codes.shape
    ranges = local // OWN
    hit = ranges[:, :, None, :] == jnp.arange(Y, dtype=jnp.int32)[None, None, :, None]
    hit = hit.reshape(blocks, X * Y, length)
    lane = jnp.arange(length)
    upper = (lane[:, None] < lane[None, :]).astype(jnp.bfloat16)
    rank = lax.dot_general(
        hit.astype(jnp.bfloat16).reshape(blocks * X * Y, length),
        upper,
        NN,
        preferred_element_type=jnp.float32,
    )
    rank = jnp.where(hit, rank.reshape(hit.shape).astype(jnp.int32), -1)
    slots = jnp.arange(CAP, dtype=jnp.int32)
    chosen = (rank[:, :, None, :] == slots[None, None, :, None]).astype(jnp.bfloat16)
    chosen = chosen.reshape(blocks, X * Y * CAP, length)
    ones = jnp.ones_like(all_codes[:, :1])
    digits = jnp.concatenate([all_codes // BLK, all_codes % BLK, ones], axis=1)
    digits = digits.astype(jnp.bfloat16)
    packed = lax.dot_general(
        digits, chosen, (((2,), (2,)), ((0,), (0,))), preferred_element_type=jnp.float32
    ).astype(jnp.int32)
    high, low = packed[:, :codebooks], packed[:, codebooks : 2 * codebooks]
    tuples = jnp.where(packed[:, 2 * codebooks :] > 0, high * BLK + low, -1)
    tuples = tuples.reshape(blocks, codebooks, X, Y * CAP)
    return tuples.transpose(2, 1, 0, 3)


def match(index_row, count):
    ids = lax.broadcasted_iota(jnp.int32, (count, index_row.shape[1]), 0)
    return jnp.where(ids == index_row, 1.0, 0.0).astype(jnp.bfloat16)


def weight_kernel(row_ref, column_ref, vector_ref, out_ref):
    member = match(row_ref[0], PLANE)
    out_ref[...] = match(vector_ref[0], PLANE)
    for core in range(C):
        table = match(column_ref[0, core : core + 1, :], Z * OWN)
        counts = lax.dot_general(member, table, NT, preferred_element_type=jnp.float32)
        counts = (-counts).astype(out_ref.dtype)
        for z in range(Z):
            start = (core * Z + z) * (OWN + HALF)
            out_ref[:, start : start + OWN] = counts[:, z * OWN : (z + 1) * OWN]


def weights(row_index, column_index, vector_index):
    books, _, slots = row_index.shape
    columns = vector_index.shape[2]
    return pl.pallas_call(
        weight_kernel,
        grid=(books,),
        in_specs=[
            pl.BlockSpec((1, 1, slots), lambda i: (i, 0, 0)),
            pl.BlockSpec((1, C, slots), lambda i: (i, 0, 0)),
            pl.BlockSpec((1, 1, columns), lambda i: (i, 0, 0)),
        ],
        out_specs=pl.BlockSpec((PLANE, columns), lambda i: (i, 0)),
        out_shape=jax.ShapeDtypeStruct((books * PLANE, columns), jnp.bfloat16),
        compiler_params=pltpu.CompilerParams(vmem_limit_bytes=56 << 20),
        name="weights",
    )(row_index, column_index, vector_index)


def product_kernel(left_ref, right_ref, out_ref, table_ref, rows_ref, sems):
    parts, _, width = rows_ref.shape
    height = table_ref.shape[0] // BANDS
    bands = [slice(m * height, (m + 1) * height) for m in range(BANDS)]
    tables = [
        pltpu.make_async_copy(
            left_ref.at[pl.ds(m * height, height)],
            table_ref.at[pl.ds(m * height, height)],
            sems.at[m],
        )
        for m in range(BANDS)
    ]
    rows = [
        pltpu.make_async_copy(
            right_ref.at[:, pl.ds(n * width, width)], rows_ref.at[n], sems.at[BANDS + n]
        )
        for n in range(parts)
    ]
    for copy in rows[:1] + tables + rows[1:]:
        copy.start()
    for n in range(parts):
        rows[n].wait()
        for m, band in enumerate(bands):
            if n == 0:
                tables[m].wait()
            total = lax.dot_general(
                table_ref[band, :], rows_ref[n], NN, preferred_element_type=jnp.float32
            )
            out_ref[band, n * width : (n + 1) * width] = total.astype(out_ref.dtype)


def product(left, right):
    features = right.shape[1]
    parts = 2
    left, right = (pltpu.with_memory_space_constraint(a, pltpu.HBM) for a in (left, right))
    return pl.pallas_call(
        product_kernel,
        in_specs=[pl.BlockSpec(memory_space=pltpu.HBM)] * 2,
        out_specs=pl.BlockSpec(memory_space=pltpu.VMEM),
        out_shape=jax.ShapeDtypeStruct((left.shape[0], features), jnp.bfloat16),
        scratch_shapes=[
            pltpu.VMEM(left.shape, left.dtype),
            pltpu.VMEM((parts, right.shape[0], features // parts), right.dtype),
            pltpu.SemaphoreType.DMA((BANDS + parts,)),
        ],
        compiler_params=pltpu.CompilerParams(vmem_limit_bytes=32 << 20),
        name="product",
    )(left, right)


def piece_kernel(index_ref, book_ref, vector_ref, out_ref):
    out_ref[:OWN, :] = book_ref[...]
    out_ref[OWN:, :] = vector_ref[...]


def make_piece(book_rows, vectors, index):
    features = vectors.shape[1]
    return pl.pallas_call(
        piece_kernel,
        grid_spec=pltpu.PrefetchScalarGridSpec(
            num_scalar_prefetch=1,
            grid=(1,),
            in_specs=[
                pl.BlockSpec((OWN, features), lambda i, n: (0, 0)),
                pl.BlockSpec((HALF, features), lambda i, n: (n[0], 0)),
            ],
            out_specs=pl.BlockSpec((OWN + HALF, features), lambda i, n: (0, 0)),
        ),
        out_shape=jax.ShapeDtypeStruct((OWN + HALF, features), jnp.bfloat16),
        compiler_params=pltpu.CompilerParams(vmem_limit_bytes=4 << 20),
        name="make_piece",
    )(index, book_rows, vectors)


def gram_kernel(book_ref, start_ref, row_ref, codes_ref, out_ref):
    group = pl.program_id(0)
    member = match(row_ref[...], OWN)
    per_step = out_ref.shape[1] // BLK
    for j in range(per_step):
        p = group * per_step + j
        offset = codes_ref[pl.ds(book_ref[p], 1), :] - start_ref[p]
        out_ref[:, j * BLK : (j + 1) * BLK] = lax.dot_general(
            member, match(offset, BLK), NT, preferred_element_type=jnp.float32
        )


def gram_counts(partner_book, partner_start, row_index, tuples):
    slots = tuples.shape[1]
    width = 8 * BLK
    return pl.pallas_call(
        gram_kernel,
        grid_spec=pltpu.PrefetchScalarGridSpec(
            num_scalar_prefetch=2,
            grid=(P_SIZE * BLK // width,),
            in_specs=[
                pl.BlockSpec((1, slots), lambda g, b, s: (0, 0)),
                pl.BlockSpec(tuples.shape, lambda g, b, s: (0, 0)),
            ],
            out_specs=pl.BlockSpec((OWN, width), lambda g, b, s: (0, g)),
        ),
        out_shape=jax.ShapeDtypeStruct((OWN, P_SIZE * BLK), jnp.float32),
        compiler_params=pltpu.CompilerParams(vmem_limit_bytes=12 << 20),
        name="gram_counts",
    )(partner_book, partner_start, row_index, tuples)


def by_parity(rows, core):
    shape = rows.shape
    grouped = rows.reshape(shape[:-2] + (X, C, shape[-1]))
    return lax.dynamic_index_in_dim(grouped, core, len(shape) - 1, keepdims=False)


def slot_indices(tuples, z, y, x, core):
    own = jnp.stack(
        [lax.dynamic_index_in_dim(tuples[i], i * C + core, 0, keepdims=True) for i in range(X)]
    )
    row_index = jnp.where(own >= 0, own - PLANE * z, -1)
    code = lax.dynamic_slice_in_dim(tuples, x * C, C, 1)
    place = code // PLANE * OWN + code % OWN
    inside = (code >= 0) & (code // OWN % Y == y)
    return row_index, jnp.where(inside, place, -1)


def vector_rows(all_codes, z, y, x, core):
    mine = all_codes.reshape(Z, Y, X * C, -1)
    mine = lax.dynamic_index_in_dim(mine, y, 1, keepdims=False)
    portion = lax.dynamic_slice_in_dim(mine, C * HALF * x, C * HALF, 2)
    portion = by_parity(portion, core).reshape(Z, X, C, HALF) - PLANE * z
    portion = jnp.pad(
        portion.transpose(1, 2, 0, 3), ((0, 0), (0, 0), (0, 0), (OWN, 0)), constant_values=-1
    )
    return portion.reshape(X, 1, Z * C * (OWN + HALF))


def shards(vectors, codes, codebook, pairs):
    z, y = lax.axis_index("z"), lax.axis_index("y")
    x, core = lax.axis_index("x"), lax.axis_index("core")
    features = codebook.shape[2]
    owner = z * Y + y
    book = x * C + core
    stored = (pltpu.with_memory_space_constraint(a, pltpu.HBM) for a in (codebook[0], vectors))
    piece = make_piece(*stored, book.astype(jnp.int32)[None])
    rows = lax.all_gather(piece, ("core", "z"), tiled=True)
    all_codes = gather_codes(codes, book)
    local = by_parity(all_codes, core) - PLANE * z
    tuples = compact(all_codes, local)
    tuples = tuples.reshape(X, tuples.shape[1], -1)
    row_index, column_index = slot_indices(tuples, z, y, x, core)
    table = weights(row_index, column_index, vector_rows(all_codes, z, y, x, core))
    held = lax.dynamic_index_in_dim(tuples, x, 0, keepdims=False)
    held = held.reshape(X * C, -1, Y, CAP)
    held = lax.dynamic_index_in_dim(held, y, 2, keepdims=False).reshape(X * C, -1)
    own_row = lax.dynamic_index_in_dim(held, book, 0, keepdims=True)
    own_row = jnp.where(own_row >= 0, own_row - owner * OWN, -1)
    matched = own_row == jnp.arange(OWN, dtype=jnp.int32)[:, None]
    code_count = jnp.sum(matched.astype(jnp.float32), axis=1)
    divisor = jnp.broadcast_to(code_count[:, None] + 2.0, (OWN, features))
    current = codebook[0].astype(jnp.float32)
    base = current - 2.0 * current / divisor
    partner = lax.dynamic_index_in_dim(pairs, (book * K + owner * OWN) // BLK, 0, keepdims=False)
    gram = gram_counts(partner // KB, partner % KB * BLK, own_row, held)
    table, gram, divisor, base = lax.optimization_barrier((table, gram, divisor, base))
    partial = product(table, rows)
    partial = partial.reshape(X * Y, OWN, features)
    received = lax.all_to_all(partial, ("x", "y"), split_axis=0, concat_axis=0, tiled=True)
    right_side = jnp.sum(received.astype(jnp.float32), axis=0)
    return (base + right_side / divisor)[None], gram[None]


def solution(mesh):
    grid = Mesh(mesh.devices.reshape(Z, Y, X, C), ("z", "y", "x", "core"))
    rows, books = ("z", "y"), ("x", "core")
    in_specs = (P(rows, None), P(None, rows), P(books, rows, None), P())
    out_specs = (P(books, rows, None), P(books, rows, None))
    return jax.shard_map(shards, mesh=grid, in_specs=in_specs, out_specs=out_specs, check_vma=False)
```

```python
import jax
import jax.numpy as jnp
from jax import lax
from jax.experimental import pallas as pl
from jax.experimental.pallas import tpu as pltpu
from jax.sharding import Mesh, PartitionSpec as P

K = 4096
BLK = 128
P_SIZE = 64
KB = 32
Z, Y, X, C = 16, 4, 4, 2
OWN = 64
CAP = 8
BANDS = X
HALF = 32
PLANE = Y * OWN
NT = (((1,), (1,)), ((), ()))
NN = (((1,), (0,)), ((), ()))


def gather_codes(codes, book):
    mine = lax.dynamic_slice_in_dim(codes.astype(jnp.int16), book, 1, 0)
    copies = jnp.broadcast_to(mine[None], (Z * Y,) + mine.shape)
    whole = lax.all_to_all(copies, ("z", "y"), split_axis=0, concat_axis=0, tiled=True)
    whole = whole.reshape(Z * Y, codes.shape[1])
    copies = jnp.broadcast_to(whole[None], (X * C,) + whole.shape)
    books = lax.all_to_all(copies, ("x", "core"), split_axis=0, concat_axis=0, tiled=True)
    return books.astype(jnp.int32).transpose(1, 0, 2)


def compact(all_codes, local):
    blocks, codebooks, length = all_codes.shape
    ranges = local // OWN
    hit = ranges[:, :, None, :] == jnp.arange(Y, dtype=jnp.int32)[None, None, :, None]
    hit = hit.reshape(blocks, X * Y, length)
    lane = jnp.arange(length)
    upper = (lane[:, None] < lane[None, :]).astype(jnp.bfloat16)
    rank = lax.dot_general(
        hit.astype(jnp.bfloat16).reshape(blocks * X * Y, length),
        upper,
        NN,
        preferred_element_type=jnp.float32,
    )
    rank = jnp.where(hit, rank.reshape(hit.shape).astype(jnp.int32), -1)
    slots = jnp.arange(CAP, dtype=jnp.int32)
    chosen = (rank[:, :, None, :] == slots[None, None, :, None]).astype(jnp.bfloat16)
    chosen = chosen.reshape(blocks, X * Y * CAP, length)
    ones = jnp.ones_like(all_codes[:, :1])
    digits = jnp.concatenate([all_codes // BLK, all_codes % BLK, ones], axis=1)
    digits = digits.astype(jnp.bfloat16)
    packed = lax.dot_general(
        digits, chosen, (((2,), (2,)), ((0,), (0,))), preferred_element_type=jnp.float32
    ).astype(jnp.int32)
    high, low = packed[:, :codebooks], packed[:, codebooks : 2 * codebooks]
    tuples = jnp.where(packed[:, 2 * codebooks :] > 0, high * BLK + low, -1)
    tuples = tuples.reshape(blocks, codebooks, X, Y * CAP)
    return tuples.transpose(2, 1, 0, 3)


def match(index_row, count):
    ids = lax.broadcasted_iota(jnp.int32, (count, index_row.shape[1]), 0)
    return jnp.where(ids == index_row, 1.0, 0.0).astype(jnp.bfloat16)


def weight_kernel(row_ref, column_ref, vector_ref, out_ref):
    member = match(row_ref[0], PLANE)
    out_ref[...] = match(vector_ref[0], PLANE)
    for core in range(C):
        table = match(column_ref[0, core : core + 1, :], Z * OWN)
        counts = lax.dot_general(member, table, NT, preferred_element_type=jnp.float32)
        counts = (-counts).astype(out_ref.dtype)
        for z in range(Z):
            start = (core * Z + z) * (OWN + HALF)
            out_ref[:, start : start + OWN] = counts[:, z * OWN : (z + 1) * OWN]


def weights(row_index, column_index, vector_index):
    books, _, slots = row_index.shape
    columns = vector_index.shape[2]
    return pl.pallas_call(
        weight_kernel,
        grid=(books,),
        in_specs=[
            pl.BlockSpec((1, 1, slots), lambda i: (i, 0, 0)),
            pl.BlockSpec((1, C, slots), lambda i: (i, 0, 0)),
            pl.BlockSpec((1, 1, columns), lambda i: (i, 0, 0)),
        ],
        out_specs=pl.BlockSpec((PLANE, columns), lambda i: (i, 0)),
        out_shape=jax.ShapeDtypeStruct((books * PLANE, columns), jnp.bfloat16),
        compiler_params=pltpu.CompilerParams(vmem_limit_bytes=56 << 20),
        name="weights",
    )(row_index, column_index, vector_index)


def product_kernel(left_ref, right_ref, out_ref, table_ref, rows_ref, sems):
    parts, _, width = rows_ref.shape
    height = table_ref.shape[0] // BANDS
    bands = [slice(m * height, (m + 1) * height) for m in range(BANDS)]
    tables = [
        pltpu.make_async_copy(
            left_ref.at[pl.ds(m * height, height)],
            table_ref.at[pl.ds(m * height, height)],
            sems.at[m],
        )
        for m in range(BANDS)
    ]
    rows = [
        pltpu.make_async_copy(
            right_ref.at[:, pl.ds(n * width, width)], rows_ref.at[n], sems.at[BANDS + n]
        )
        for n in range(parts)
    ]
    for copy in rows[:1] + tables + rows[1:]:
        copy.start()
    for n in range(parts):
        rows[n].wait()
        for m, band in enumerate(bands):
            if n == 0:
                tables[m].wait()
            total = lax.dot_general(
                table_ref[band, :], rows_ref[n], NN, preferred_element_type=jnp.float32
            )
            total = total.astype(out_ref.dtype)
            for y in range(Y):
                start = (y * X + m) * OWN
                out_ref[start : start + OWN, n * width : (n + 1) * width] = total[
                    y * OWN : (y + 1) * OWN, :
                ]


def product(left, right):
    features = right.shape[1]
    parts = 2
    left, right = (pltpu.with_memory_space_constraint(a, pltpu.HBM) for a in (left, right))
    return pl.pallas_call(
        product_kernel,
        in_specs=[pl.BlockSpec(memory_space=pltpu.HBM)] * 2,
        out_specs=pl.BlockSpec(memory_space=pltpu.VMEM),
        out_shape=jax.ShapeDtypeStruct((left.shape[0], features), jnp.bfloat16),
        scratch_shapes=[
            pltpu.VMEM(left.shape, left.dtype),
            pltpu.VMEM((parts, right.shape[0], features // parts), right.dtype),
            pltpu.SemaphoreType.DMA((BANDS + parts,)),
        ],
        compiler_params=pltpu.CompilerParams(vmem_limit_bytes=32 << 20),
        name="product",
    )(left, right)


def piece_kernel(index_ref, book_ref, vector_ref, out_ref):
    out_ref[:OWN, :] = book_ref[...]
    out_ref[OWN:, :] = vector_ref[...]


def make_piece(book_rows, vectors, index):
    features = vectors.shape[1]
    return pl.pallas_call(
        piece_kernel,
        grid_spec=pltpu.PrefetchScalarGridSpec(
            num_scalar_prefetch=1,
            grid=(1,),
            in_specs=[
                pl.BlockSpec((OWN, features), lambda i, n: (0, 0)),
                pl.BlockSpec((HALF, features), lambda i, n: (n[0], 0)),
            ],
            out_specs=pl.BlockSpec((OWN + HALF, features), lambda i, n: (0, 0)),
        ),
        out_shape=jax.ShapeDtypeStruct((OWN + HALF, features), jnp.bfloat16),
        compiler_params=pltpu.CompilerParams(vmem_limit_bytes=4 << 20),
        name="make_piece",
    )(index, book_rows, vectors)


def gram_kernel(book_ref, start_ref, row_ref, codes_ref, out_ref):
    group = pl.program_id(0)
    member = match(row_ref[...], OWN)
    per_step = out_ref.shape[1] // BLK
    for j in range(per_step):
        p = group * per_step + j
        offset = codes_ref[pl.ds(book_ref[p], 1), :] - start_ref[p]
        out_ref[:, j * BLK : (j + 1) * BLK] = lax.dot_general(
            member, match(offset, BLK), NT, preferred_element_type=jnp.float32
        )


def gram_counts(partner_book, partner_start, row_index, tuples):
    slots = tuples.shape[1]
    width = 8 * BLK
    return pl.pallas_call(
        gram_kernel,
        grid_spec=pltpu.PrefetchScalarGridSpec(
            num_scalar_prefetch=2,
            grid=(P_SIZE * BLK // width,),
            in_specs=[
                pl.BlockSpec((1, slots), lambda g, b, s: (0, 0)),
                pl.BlockSpec(tuples.shape, lambda g, b, s: (0, 0)),
            ],
            out_specs=pl.BlockSpec((OWN, width), lambda g, b, s: (0, g)),
        ),
        out_shape=jax.ShapeDtypeStruct((OWN, P_SIZE * BLK), jnp.float32),
        compiler_params=pltpu.CompilerParams(vmem_limit_bytes=12 << 20),
        name="gram_counts",
    )(partner_book, partner_start, row_index, tuples)


def by_parity(rows, core):
    shape = rows.shape
    grouped = rows.reshape(shape[:-2] + (X, C, shape[-1]))
    return lax.dynamic_index_in_dim(grouped, core, len(shape) - 1, keepdims=False)


def slot_indices(tuples, z, y, x, core):
    own = jnp.stack(
        [lax.dynamic_index_in_dim(tuples[i], i * C + core, 0, keepdims=True) for i in range(X)]
    )
    row_index = jnp.where(own >= 0, own - PLANE * z, -1)
    code = lax.dynamic_slice_in_dim(tuples, x * C, C, 1)
    place = code // PLANE * OWN + code % OWN
    inside = (code >= 0) & (code // OWN % Y == y)
    return row_index, jnp.where(inside, place, -1)


def vector_rows(all_codes, z, y, x, core):
    mine = all_codes.reshape(Z, Y, X * C, -1)
    mine = lax.dynamic_index_in_dim(mine, y, 1, keepdims=False)
    portion = lax.dynamic_slice_in_dim(mine, C * HALF * x, C * HALF, 2)
    portion = by_parity(portion, core).reshape(Z, X, C, HALF) - PLANE * z
    portion = jnp.pad(
        portion.transpose(1, 2, 0, 3), ((0, 0), (0, 0), (0, 0), (OWN, 0)), constant_values=-1
    )
    return portion.reshape(X, 1, Z * C * (OWN + HALF))


def shards(vectors, codes, codebook, pairs):
    z, y = lax.axis_index("z"), lax.axis_index("y")
    x, core = lax.axis_index("x"), lax.axis_index("core")
    features = codebook.shape[2]
    owner = z * Y + y
    book = x * C + core
    stored = (pltpu.with_memory_space_constraint(a, pltpu.HBM) for a in (codebook[0], vectors))
    piece = make_piece(*stored, book.astype(jnp.int32)[None])
    rows = lax.all_gather(piece, ("core", "z"), tiled=True)
    all_codes = gather_codes(codes, book)
    local = by_parity(all_codes, core) - PLANE * z
    tuples = compact(all_codes, local)
    tuples = tuples.reshape(X, tuples.shape[1], -1)
    row_index, column_index = slot_indices(tuples, z, y, x, core)
    table = weights(row_index, column_index, vector_rows(all_codes, z, y, x, core))
    held = lax.dynamic_index_in_dim(tuples, x, 0, keepdims=False)
    held = held.reshape(X * C, -1, Y, CAP)
    held = lax.dynamic_index_in_dim(held, y, 2, keepdims=False).reshape(X * C, -1)
    own_row = lax.dynamic_index_in_dim(held, book, 0, keepdims=True)
    own_row = jnp.where(own_row >= 0, own_row - owner * OWN, -1)
    matched = own_row == jnp.arange(OWN, dtype=jnp.int32)[:, None]
    code_count = jnp.sum(matched.astype(jnp.float32), axis=1)
    divisor = jnp.broadcast_to(code_count[:, None] + 2.0, (OWN, features))
    current = codebook[0].astype(jnp.float32)
    base = current - 2.0 * current / divisor
    partner = lax.dynamic_index_in_dim(pairs, (book * K + owner * OWN) // BLK, 0, keepdims=False)
    gram = gram_counts(partner // KB, partner % KB * BLK, own_row, held)
    table, gram, divisor, base = lax.optimization_barrier((table, gram, divisor, base))
    partial = product(table, rows)
    partial = partial.reshape(X * Y, OWN, features)
    received = lax.all_to_all(partial, ("y", "x"), split_axis=0, concat_axis=0, tiled=True)
    right_side = jnp.sum(received.astype(jnp.float32), axis=0)
    return (base + right_side / divisor)[None], gram[None]


def solution(mesh):
    grid = Mesh(mesh.devices.reshape(Z, Y, X, C), ("z", "y", "x", "core"))
    rows, books = ("z", "y"), ("x", "core")
    in_specs = (P(rows, None), P(None, rows), P(books, rows, None), P())
    out_specs = (P(books, rows, None), P(books, rows, None))
    return jax.shard_map(shards, mesh=grid, in_specs=in_specs, out_specs=out_specs, check_vma=False)
```
